32 devices in a mesh: axial: 8 (over y, x, core), azim: 4 (over z).
Axes of the slice: x: 2, y: 2, z: 4, core: 2. Of those that a mesh axis runs over, the one named last changes fastest.
Arguments:
- displace: float32 [3, 128, 12, 512], P(None, 'axial', None, 'azim'), may hold values from -6 to 6
- velocity: float32 [3, 128, 12, 512], P(None, 'axial', None, 'azim'), may hold values from -4 to 4
- micro_modulus_values: float32 [128, 12, 512], P('axial', None, 'azim'), may hold values from 0.5 to 2
- thermal: float32 [192, 512], P('axial', 'azim'), may hold values from 0 to 2
- owner_of: int32 [8, 4, 48, 1], P('axial', 'azim'), may hold values from 0 to 7; in each aligned block of 48 rows (0 to 47, 48 to 95, ..., all dimensions but the last counted through in order) at most 12 rows name the same one
- row_of: int32 [8, 4, 48], P('axial', 'azim'), may hold values from 0 to 23
- breaks: int32 [4, 8, 4, 512], P(None, 'axial', 'azim'), may hold values from 0 to 368639, as said below
Outputs:
- disp_out: float32 [3, 128, 12, 512], P(None, 'axial', None, 'azim')
- veloc_out: float32 [3, 128, 12, 512], P(None, 'axial', None, 'azim')
- heat_source: float32 [192, 512], P('axial', 'azim')
The draws below stay inside these ranges and needn't reach their ends.
Inputs may be any that keep to these rules, and one draw needn't show every extreme that they name: `owner_of`: among the 48 requests of one device, no owner is named more than 12 times, a bound that some block reaches. `breaks`: A code names a half-offset and a particle of the listing device as in the reference program; a code of half-offset 14 at the last radial layer names no bond. Codes may repeat.
All inputs are finite; a program needn't handle non-finite values.
Results may differ from the reference program's by a relative error of at most 0.00011.
Values sent between devices are 32-bit elements; how exact they have to be, the bound alone decides.
No kernel may reach another device: no remote copies, remote signals or barrier semaphores. Data moves between devices by JAX's collectives and lax.ppermute only.
A program may use at most 128 MiB of HBM per device.

```python
import math
import jax
import jax.numpy as jnp
import numpy as np

CA = 16
CZ = 128
SHELL_TIERS = 12
STEPS = 4
BREAKS = 512
NREQ = 48
TROWS_DEV = 24
CAP = 12
LONGITUDE_SITES = 128
ANGULAR_SITES = 512
THROWS = 192
N_AXIAL = 8
N_AZIM = 4


def draw_breaks(key, part):
    shape = (STEPS, N_AXIAL, N_AZIM, BREAKS)
    subkeys = jax.random.split(jax.random.fold_in(key, 41), 7)
    bond_kind = jax.random.randint(subkeys[0], shape, 0, 15)
    choose_mode = jax.random.randint(subkeys[1], shape, 0, 4)
    axial_any = jax.random.randint(subkeys[2], shape, 0, CA)
    axial_raw = jax.random.randint(subkeys[3], shape, 0, 6)
    axial_edge = jnp.where(axial_raw < 3, axial_raw, CA - 6 + axial_raw)
    azim_any = jax.random.randint(subkeys[4], shape, 0, CZ)
    azim_raw = jax.random.randint(subkeys[5], shape, 0, 6)
    azim_edge = jnp.where(azim_raw < 3, azim_raw, CZ - 6 + azim_raw)
    layer_pick = jax.random.randint(subkeys[6], shape, 0, SHELL_TIERS)
    pos_a = jnp.where(choose_mode == 2, axial_edge, axial_any)
    pos_z = jnp.where(choose_mode == 3, azim_edge, azim_any)
    codes = bond_kind * (CA * SHELL_TIERS * CZ) + pos_a * (SHELL_TIERS * CZ) + layer_pick * CZ + pos_z
    return codes.astype(jnp.int32)


def set_ends(drawn, rng, low, largest):
    dims = drawn.shape
    place = [jax.random.randint(jax.random.fold_in(rng, axis), (), 0, dims[axis]) for axis in range(len(dims))]
    drawn = drawn.at[tuple(place)].set(low)
    longest = dims.index(max(dims))
    place[longest] = (place[longest] + 1) % dims[longest]
    return drawn.at[tuple(place)].set(largest)


def levels(own_key, shape, pieces, least, top_value):
    def one(position, shards_of):
        steps = jax.random.uniform(jax.random.fold_in(jax.random.fold_in(own_key, 6), position), (shards_of,), jnp.float32, least / len(pieces), top_value / len(pieces))
        return jnp.repeat(jnp.exp(steps), shape[position] // shards_of).reshape((-1,) + (1,) * (len(shape) - position - 1))

    factor_of = one(*pieces[0])
    for cut in pieces[1:]:
        factor_of = factor_of * one(*cut)
    return factor_of


def routed_block(stream_key, own, number, rows, number_of, top, reach, skew):
    sequence = jax.random.permutation(stream_key, number_of)
    packed, ordinary = load_shares(number_of, rows * top, reach, skew, True), load_shares(number_of, rows * top, reach, skew, False)
    places = jnp.arange(number_of)

    def named(lengths, turn):
        used = int((lengths > 0).sum())
        fixed = max(1, used // 4)
        shifted = fixed + (places - fixed + turn * (used - fixed)) % max(1, number_of - fixed)
        return jnp.zeros((number_of,), jnp.int32).at[sequence[jnp.where(places < fixed, places, shifted)]].set(jnp.asarray(lengths, jnp.int32))

    lengths = jnp.where(number % 4 == 0, named(packed, number // 4), named(ordinary, number - number // 4 - 1))
    mixed = jax.random.permutation(jax.random.fold_in(own, 3), number_of)
    donor, receiver = mixed[0:number_of // 2 * 2:2], mixed[1:number_of // 2 * 2:2]
    room = jnp.minimum(lengths[donor] - 1, reach - lengths[receiver]) // 2
    room = jnp.where((donor == sequence[0]) | (receiver == sequence[0]) | (lengths[receiver] == 0), 0, jnp.maximum(room, 0))
    shifted = jax.random.randint(jax.random.fold_in(own, 4), (number_of // 2,), 0, 1 << 20) % (room + 1)
    lengths = lengths.at[donor].add(-shifted).at[receiver].add(shifted)
    labels = jnp.searchsorted(jnp.cumsum(lengths), jnp.arange(rows * top), side="right").astype(jnp.int32)
    grid = labels.reshape(top, rows).T
    grid = grid[jax.random.permutation(jax.random.fold_in(own, 1), rows)]
    turn = jax.random.randint(jax.random.fold_in(own, 2), (rows, 1), 0, top)
    return jnp.take_along_axis(grid, (jnp.arange(top)[None, :] + turn) % top, axis=1)


def load_shares(amount, total, bound, slope, full):
    portions = [(1 << 20) // math.isqrt(grade ** slope) + 1 for grade in range(1, amount + 1)]
    largest = bound if full else min(bound, max(-(-total // amount), total * portions[0] // sum(portions)))
    least = 1 if total - largest >= amount - 1 else 0
    counts, spare = [largest] + [least] * (amount - 1), total - largest - least * (amount - 1)
    while spare > 0:
        candidates = [i for i in range(1, amount) if counts[i] < largest] or [i for i in range(1, amount) if counts[i] < bound]
        mass, left = sum([portions[i] for i in candidates]), spare
        for i in candidates:
            extra = min(bound - counts[i], max(1, left * portions[i] // mass), spare)
            counts[i] = counts[i] + extra
            spare = spare - extra
    return np.array(counts)


def bell_draw(key, extent, scale, most, pieces=(), held_as=jnp.bfloat16):
    gain = levels(key, extent, pieces, -0.22, 0.18) if pieces else 1.0
    result = jax.random.normal(key, extent, jnp.float32) * scale * gain
    return jnp.minimum(jnp.maximum(result, -most), most).astype(held_as)


def setup_inputs(seed: int = 0) -> dict:
    keys = jax.random.split(jax.random.key(seed), 8)
    displace = bell_draw(keys[0], (3, LONGITUDE_SITES, SHELL_TIERS, ANGULAR_SITES), 1.0, 6.0, ((1, 8), (3, 4)), jnp.float32)
    velocity = bell_draw(keys[1], (3, LONGITUDE_SITES, SHELL_TIERS, ANGULAR_SITES), 0.5, 4.0, ((1, 8), (3, 4)), jnp.float32)
    micro_modulus_values = jnp.clip(jnp.exp(math.log(2.0) - 1.3862944 * jax.random.uniform(keys[2], (LONGITUDE_SITES, SHELL_TIERS, ANGULAR_SITES), jnp.float32) ** levels(keys[2], (LONGITUDE_SITES, SHELL_TIERS, ANGULAR_SITES), ((0, 8), (2, 4)), -0.2, 0.2)), 0.5, 2.0)
    thermal = jnp.clip(2.0 * jax.random.uniform(keys[3], (THROWS, ANGULAR_SITES), jnp.float32) ** levels(keys[3], (THROWS, ANGULAR_SITES), ((0, 8), (1, 4)), -0.2, 0.2), 0.0, 2.0)
    owner_of_keys = jax.random.split(jax.random.fold_in(keys[4], 1), N_AXIAL * N_AZIM * NREQ // NREQ)
    owner_of_turns = jax.random.permutation(jax.random.fold_in(keys[4], 3), N_AXIAL * N_AZIM * NREQ // NREQ)
    owner_of = jax.vmap(lambda own, number: routed_block(jax.random.fold_in(keys[4], 2), own, number, NREQ, N_AXIAL, 1, CAP, 2))(owner_of_keys, owner_of_turns).reshape((N_AXIAL, N_AZIM, NREQ, 1))
    row_of = set_ends(jax.random.randint(keys[5], (N_AXIAL, N_AZIM, NREQ), 0, TROWS_DEV), jax.random.fold_in(keys[5], 1), 0, TROWS_DEV - 1).astype(jnp.int32)
    breaks = draw_breaks(jax.random.fold_in(keys[7], 71), 0)
    return dict(displace=displace, velocity=velocity, micro_modulus_values=micro_modulus_values, thermal=thermal, owner_of=owner_of, row_of=row_of, breaks=breaks)


DILATION_FACTOR = 0.25
DT = 0.2

def offset_table():
    neighbor_offsets = []
    for longitude_step_by in range(4):
        for angular_step_by in range(-3, 4):
            if longitude_step_by * longitude_step_by + angular_step_by * angular_step_by <= 9 and (longitude_step_by > 0 or angular_step_by > 0):
                neighbor_offsets.append((longitude_step_by, 0, angular_step_by))
    neighbor_offsets.append((0, 1, 0))
    return neighbor_offsets

def ahead_glance(field, longitude_step_by, shell_step_by, angular_step_by):
    moved = jnp.roll(field, -angular_step_by, axis=-1)
    if shell_step_by > 0:
        moved = jnp.concatenate([moved[..., shell_step_by:, :], jnp.zeros_like(moved[..., :shell_step_by, :])], axis=-2)
    if longitude_step_by > 0:
        moved = jnp.concatenate([moved[..., longitude_step_by:, :, :], jnp.zeros_like(moved[..., :longitude_step_by, :, :])], axis=-3)
    return moved

def look_behind(field, longitude_step_by, shell_step_by, angular_step_by):
    moved = jnp.roll(field, angular_step_by, axis=-1)
    if shell_step_by > 0:
        moved = jnp.concatenate([jnp.zeros_like(moved[..., :shell_step_by, :]), moved[..., :-shell_step_by, :]], axis=-2)
    if longitude_step_by > 0:
        moved = jnp.concatenate([jnp.zeros_like(moved[..., :longitude_step_by, :, :]), moved[..., :-longitude_step_by, :, :]], axis=-3)
    return moved

def reference(displace, velocity, micro_modulus_values, thermal, owner_of, row_of, breaks):
    neighbor_offsets = offset_table()
    wanted = (owner_of[..., 0] * TROWS_DEV + row_of).astype(jnp.int32)
    table_rows = thermal.reshape(THROWS, N_AZIM, CZ)
    column = jnp.arange(N_AZIM, dtype=jnp.int32).reshape(1, N_AZIM, 1)
    blocky_heat_grid = table_rows[wanted, column]
    blocky_heat_grid = blocky_heat_grid.reshape(N_AXIAL, N_AZIM, CA // 2, SHELL_TIERS // 2, CZ)
    detailed_particle_grid = jnp.repeat(jnp.repeat(blocky_heat_grid, 2, axis=2), 2, axis=3)
    heat_level_values = detailed_particle_grid.transpose(0, 2, 3, 1, 4).reshape(LONGITUDE_SITES, SHELL_TIERS, ANGULAR_SITES)
    bond_stride = CA * SHELL_TIERS * CZ
    bond_kind = breaks // bond_stride
    remainder = breaks % bond_stride
    pos_z = remainder % CZ
    pos_r = remainder // CZ % SHELL_TIERS
    pos_a = remainder // (SHELL_TIERS * CZ)
    glob_a = jnp.arange(N_AXIAL, dtype=jnp.int32).reshape(1, N_AXIAL, 1, 1) * CA + pos_a
    glob_z = jnp.arange(N_AZIM, dtype=jnp.int32).reshape(1, 1, N_AZIM, 1) * CZ + pos_z
    unbroken_bonds = jnp.ones((15, LONGITUDE_SITES, SHELL_TIERS, ANGULAR_SITES), bool)
    filled = jnp.ones((LONGITUDE_SITES, SHELL_TIERS, ANGULAR_SITES), micro_modulus_values.dtype)
    disp, veloc = (displace, velocity)
    summed = jnp.zeros((LONGITUDE_SITES, SHELL_TIERS, ANGULAR_SITES), micro_modulus_values.dtype)
    for section_index in range(STEPS):
        unbroken_bonds = unbroken_bonds.at[bond_kind[section_index], glob_a[section_index], pos_r[section_index], glob_z[section_index]].set(False)
        forces = [jnp.zeros((LONGITUDE_SITES, SHELL_TIERS, ANGULAR_SITES), micro_modulus_values.dtype) for component in range(3)]
        for number, offset in enumerate(neighbor_offsets):
            longitude_step_by, shell_step_by, angular_step_by = offset
            link_rest_span = math.sqrt(longitude_step_by * longitude_step_by + shell_step_by * shell_step_by + angular_step_by * angular_step_by)
            link_elongation = 0.0
            for component in range(3):
                if offset[component] != 0:
                    link_elongation = link_elongation + offset[component] * (ahead_glance(disp[component], longitude_step_by, shell_step_by, angular_step_by) - disp[component])
            link_relative_stretch = link_elongation / (link_rest_span * link_rest_span) - DILATION_FACTOR * 0.5 * (ahead_glance(heat_level_values, longitude_step_by, shell_step_by, angular_step_by) + heat_level_values)
            exists = ahead_glance(filled, longitude_step_by, shell_step_by, angular_step_by)
            bond_force = 0.5 * (ahead_glance(micro_modulus_values, longitude_step_by, shell_step_by, angular_step_by) + micro_modulus_values) * unbroken_bonds[number].astype(micro_modulus_values.dtype) * exists * link_relative_stretch / link_rest_span
            net_term = bond_force - look_behind(bond_force, longitude_step_by, shell_step_by, angular_step_by)
            for component in range(3):
                if offset[component] != 0:
                    forces[component] = forces[component] + net_term * (offset[component] / link_rest_span)
            summed = summed + 0.5 * bond_force * link_relative_stretch
        veloc = veloc + DT * jnp.stack(forces)
        disp = disp + DT * veloc
    pooled = summed.reshape(N_AXIAL, CA // 2, 2, SHELL_TIERS // 2, 2, N_AZIM, CZ).mean(axis=(2, 4)) / STEPS
    pooled = pooled.transpose(0, 3, 1, 2, 4).reshape(N_AXIAL, N_AZIM, NREQ, CZ)
    heat = jnp.zeros((THROWS, N_AZIM, CZ), micro_modulus_values.dtype).at[wanted, column].add(pooled)
    return (disp, veloc, heat.reshape(THROWS, ANGULAR_SITES))
```

```python
import math

import jax
import jax.numpy as jnp
from jax import lax
from jax.experimental import pallas as pl
from jax.experimental.pallas import tpu as pltpu
from jax.sharding import PartitionSpec as P

DILATION = 0.25
DT = 0.2
CA, NR, CZ = 16, 12, 128
REACH = 3
SLOT = 16
PAIR = 2 * NR
NFIELD = 7
NEXACT = lax.Precision.HIGHEST
F32 = jnp.float32


def offset_table():
    table = []
    for da in range(REACH + 1):
        for dz in range(-REACH, REACH + 1):
            if da * da + dz * dz <= REACH * REACH and (da > 0 or dz > 0):
                table.append((da, 0, dz))
    table.append((0, 1, 0))
    return table


OFFSETS = offset_table()
NBOND = len(OFFSETS)
NUMBER = {o: i for i, o in enumerate(OFFSETS)}


def scales(o):
    return sum(x * x for x in o), math.gcd(math.gcd(o[0], o[1]), abs(o[2]))


def roll(x, shift, axis=1):
    shift %= x.shape[axis]
    return pltpu.roll(x, shift, axis) if shift else x


def lanes_of(shape=(NR, CZ)):
    return lax.broadcasted_iota(jnp.int32, shape, 1)


def dot_nt(a, b):
    return lax.dot_general(a, b, (((1,), (1,)), ((), ())), preferred_element_type=F32)


class Sizes:
    def __init__(self, sections):
        self.sections = sections
        self.halo = REACH * sections
        self.ext = CA + 2 * self.halo
        self.code_at = NFIELD * self.halo * NR
        self.code_rows = sections * 4
        self.tab_at = self.code_at + self.code_rows
        self.tab_rows = CA // 2 * NR
        self.edge_rows = self.tab_at + self.tab_rows
        self.tiles = self.ext * SLOT // CZ
        self.strip_code_at = (NFIELD + 1) * self.tiles * NR
        self.strip_rows = self.strip_code_at + 3 * self.code_rows

    def source(self, a):
        if a < self.halo:
            return 0, CA - self.halo + a, a
        if a < self.halo + CA:
            return 1, a - self.halo, None
        return 2, a - self.halo - CA, a - self.halo - CA


def own_plane(refs, f, a):
    disp, velo, stiff = refs
    if f < 3:
        return disp[f, a]
    if f < 6:
        return velo[f - 3, a]
    return stiff[a]


def field_plane(sz, refs, low, high, temp, f, a):
    if f == NFIELD:
        return temp[pl.ds(a // 2 * NR, NR), :]
    which, there, edge = sz.source(a)
    if which == 1:
        return own_plane(refs, f, there)
    src = low if which == 0 else high
    return src[pl.ds((f * sz.halo + edge) * NR, NR), :]


def pack_axial(sz, disp, velo, stiff, codes, table, up, down):
    refs = (disp, velo, stiff)
    for f in range(NFIELD):
        for i in range(sz.halo):
            at = pl.ds((f * sz.halo + i) * NR, NR)
            up[at, :] = own_plane(refs, f, CA - sz.halo + i)
            down[at, :] = own_plane(refs, f, i)
    for out in (up, down):
        out[pl.ds(sz.code_at, sz.code_rows), :] = codes[...].astype(F32)
        out[pl.ds(sz.tab_at, sz.tab_rows), :] = table[...].astype(F32)


def pack_azimuth(sz, disp, velo, stiff, codes, table, low, high, thermal, left, right, temp):
    refs = (disp, velo, stiff)
    rows = thermal.shape[0]
    at = 0
    for which in range(3):
        if which == 1:
            tab = table[...].astype(F32)
        else:
            tab = (low if which == 0 else high)[pl.ds(sz.tab_at, sz.tab_rows), :]
        column = lax.broadcasted_iota(jnp.int32, (sz.tab_rows, rows), 1).astype(F32)
        hot = (tab[:, 0:1] == column).astype(F32)
        got = jnp.dot(hot, thermal[...], precision=NEXACT, preferred_element_type=F32)
        first = (CA - sz.halo) // 2 * NR if which == 0 else 0
        count = (CA if which == 1 else sz.halo) // 2 * NR
        temp[pl.ds(at, count), :] = got[first : first + count]
        at += count
    lane = lanes_of()
    per = CZ // SLOT
    for f in range(NFIELD + 1):
        for t in range(sz.tiles):
            to_left = to_right = None
            for s in range(per):
                x = field_plane(sz, refs, low, high, temp, f, t * per + s)
                a = roll(x, SLOT * s)
                b = roll(x, SLOT * s + SLOT)
                if s == 0:
                    to_left, to_right = a, b
                else:
                    here = lane >= SLOT * s
                    to_left = jnp.where(here, a, to_left)
                    to_right = jnp.where(here, b, to_right)
            here = pl.ds((f * sz.tiles + t) * NR, NR)
            left[here, :] = to_left
            right[here, :] = to_right
    for out in (left, right):
        at = sz.strip_code_at
        n = sz.code_rows
        out[pl.ds(at, n), :] = low[pl.ds(sz.code_at, n), :]
        out[pl.ds(at + n, n), :] = codes[...].astype(F32)
        out[pl.ds(at + 2 * n, n), :] = high[pl.ds(sz.code_at, n), :]


def decode(codes):
    hi = jnp.floor(codes * (1.0 / CZ))
    z = codes - hi * CZ
    k = jnp.floor((hi + 0.5) * (1.0 / (CA * NR)))
    rest = hi - k * (CA * NR)
    a = jnp.floor((rest + 0.5) * (1.0 / NR))
    return k, a, rest - a * NR, z


def spread(ref, index, weights, rows):
    at = lax.broadcasted_iota(jnp.int32, (rows, CZ), 0).astype(F32)
    for i in range(index.shape[0]):
        w = 1.0 if weights is None else weights[i]
        ref[pl.ds(0, rows), pl.ds(i * CZ, CZ)] = jnp.where(at == index[i : i + 1, :], w, 0.0).astype(
            jnp.bfloat16
        )


def read_breaks(sz, codes, from_left, from_right, broken, rows_ref, cols_ref, main, sl, sr):
    weights = [2.0 ** (-12 * (i // 4)) for i in range(sz.code_rows)]
    lane = lanes_of()
    n = sz.code_rows * CZ
    per = CZ // SLOT
    for which in range(3):
        k, a, r, z = decode(codes[which])
        group = jnp.floor(a * 0.25)
        spread(rows_ref, k * (4 * NR) + group * NR + r, None, NBOND * 4 * NR)
        spread(cols_ref, (a - 4 * group) * CZ + z, weights, 4 * CZ)
        main[...] = dot_nt(rows_ref[...], cols_ref[...])
        for side, out in ((from_left[which], sl), (from_right[which], sr)):
            k, a, r, z = decode(side)
            if out is sl:
                slot = jnp.where(z >= CZ - SLOT, a * SLOT + z - (CZ - SLOT), -1.0)
            else:
                slot = jnp.where(z < SLOT, a * SLOT + z, -1.0)
            spread(rows_ref, k * 16 + r, None, NBOND * 16)
            spread(cols_ref, slot, weights, CA * SLOT)
            out[...] = dot_nt(
                rows_ref[pl.ds(0, NBOND * 16), :], cols_ref[pl.ds(0, CA * SLOT), :]
            )
        planes = [p for p in range(sz.ext) if sz.source(p)[0] == which]

        def place(b, carry):
            block = main[pl.ds(pl.multiple_of(b * 4 * NR, 16), 4 * NR), :]
            left = sl[pl.ds(pl.multiple_of(b * 16, 16), 16), :]
            right = sr[pl.ds(pl.multiple_of(b * 16, 16), 16), :]
            for p in planes:
                a = sz.source(p)[1]
                x = block[a // 4 * NR : a // 4 * NR + NR, a % 4 * CZ : a % 4 * CZ + CZ]
                t, s = a // per, a % per
                one = roll(left[0:NR, t * CZ : (t + 1) * CZ], SLOT - SLOT * s)
                two = roll(right[0:NR, t * CZ : (t + 1) * CZ], CZ - 2 * SLOT - SLOT * s)
                broken[b, p, pl.ds(0, NR), :] = jnp.where(lane >= 32, roll(x, 32), one)
                broken[b, p, pl.ds(NR, NR), :] = jnp.where(lane < 96, roll(x, -32), two)
            return carry

        lax.fori_loop(0, NBOND, place, 0)


def march(
    sz, total, first, disp, velo, stiff, low, high, temp, strip_l, strip_r, codes, wanted,
    out_d, out_v, out_e, fld, stiffk, heatk, broken, fa, fz, energy, rows_ref, cols_ref, main, sl, sr,
):
    refs = (disp, velo, stiff)
    lane = lanes_of()
    per = CZ // SLOT
    n = sz.code_rows
    read_breaks(
        sz,
        [low[pl.ds(sz.code_at, n), :], codes[...].astype(F32), high[pl.ds(sz.code_at, n), :]],
        [strip_l[pl.ds(sz.strip_code_at + i * n, n), :] for i in range(3)],
        [strip_r[pl.ds(sz.strip_code_at + i * n, n), :] for i in range(3)],
        broken, rows_ref, cols_ref, main, sl, sr,
    )
    for f in range(NFIELD + 1):
        for p in range(sz.ext):
            x = field_plane(sz, refs, low, high, temp, f, p)
            t, s = p // per, p % per
            here = pl.ds((f * sz.tiles + t) * NR, NR)
            one = roll(strip_l[here, :], SLOT - SLOT * s)
            two = roll(strip_r[here, :], CZ - 2 * SLOT - SLOT * s)
            fld[f, p, pl.ds(0, NR), :] = jnp.where(lane >= 32, roll(x, 32), one)
            fld[f, p, pl.ds(NR, NR), :] = jnp.where(lane < 96, roll(x, -32), two)

    row = lax.broadcasted_iota(jnp.int32, (PAIR, CZ), 0)
    not_top = jnp.where((row == NR - 1) | (row == PAIR - 1), 0.0, 1.0)
    start = first[0]

    def prepare(p, carry):
        at = start + p
        live = [
            jnp.where((at >= 0) & (at + da < total), 1.0, 0.0).astype(F32) for da in range(REACH + 1)
        ]
        for k, (da, dr, dz) in enumerate(OFFSETS):
            n2, d = scales((da, dr, dz))
            c = fld[6, p]
            h = fld[7, p]
            if dr:
                c2, h2 = roll(c, -1, 0), roll(h, -1, 0)
            else:
                c2, h2 = roll(fld[6, p + da], -dz), roll(fld[7, p + da], -dz)
            m = (c + c2) * (live[da] * (0.5 * d * d / (n2 * n2)))
            stiffk[k, p] = m * not_top if dr else m
            heatk[k, p] = (h + h2) * (DILATION * 0.5 * n2 / d)
        return carry

    last = sz.ext - REACH
    lax.fori_loop(0, last, prepare, 0)
    energy[...] = jnp.zeros_like(energy)

    def advance(p, limit, with_energy):
        ua, ur, uz = fld[0, p], fld[1, p], fld[2, p]
        sums = {}

        def bond(o, elongation):
            k = NUMBER[o]
            q = elongation - heatk[k, p]
            g = jnp.where(broken[k, p] >= limit, 0.0, stiffk[k, p]) * q
            if with_energy:
                n2 = scales(o)[0]
                sums[n2] = sums[n2] + g * q if n2 in sums else g * q
            return g

        force_a = fa[p]
        force_z = fz[p]
        for dz in (1, 2, 3):
            g = bond((0, 0, dz), roll(uz, -dz) - uz)
            force_z = force_z + (g - roll(g, dz))
        g = bond((0, 1, 0), roll(ur, -1, 0) - ur)
        force_r = g - roll(g, 1, 0)
        for da in (1, 2):
            ua2, uz2 = fld[0, p + da], fld[2, p + da]
            g = bond((da, 0, 0), ua2 - ua)
            force_a = force_a + g
            push_a = g
            push_z = None
            for dz in (1, 2):
                gs = []
                for sign in (1, -1):
                    dua = roll(ua2, -sign * dz) - ua
                    duz = roll(uz2, -sign * dz) - uz
                    if da == dz:
                        e = dua + duz if sign > 0 else dua - duz
                    elif dz == 2:
                        e = dua + (2.0 * sign) * duz
                    else:
                        e = 2.0 * dua + duz if sign > 0 else 2.0 * dua - duz
                    gs.append(bond((da, 0, sign * dz), e))
                ma = 1.0 if da == dz else float(da)
                mz = 1.0 if da == dz else float(dz)
                own_s, own_d = gs[0] + gs[1], gs[0] - gs[1]
                plus, minus = roll(gs[0], dz), roll(gs[1], -dz)
                far_s, far_d = plus + minus, plus - minus
                if ma != 1.0:
                    own_s, far_s = ma * own_s, ma * far_s
                if mz != 1.0:
                    own_d, far_d = mz * own_d, mz * far_d
                force_a = force_a + own_s
                force_z = force_z + own_d
                push_a = push_a + far_s
                push_z = far_d if push_z is None else push_z + far_d
            fa[p + da] = fa[p + da] - push_a
            fz[p + da] = fz[p + da] - push_z
        g = bond((3, 0, 0), fld[0, p + 3] - ua)
        force_a = force_a + g
        fa[p + 3] = -g
        fz[p + 3] = jnp.zeros_like(g)
        for f, u, force in ((0, ua, force_a), (1, ur, force_r), (2, uz, force_z)):
            v = fld[3 + f, p] + DT * force
            fld[3 + f, p] = v
            fld[f, p] = u + DT * v
        if with_energy:
            e = None
            for n2, x in sums.items():
                y = x * (0.5 / math.sqrt(n2))
                e = y if e is None else e + y
            energy[p - sz.halo] = energy[p - sz.halo] + e

    def step(s, limit):
        def quiet(p, c):
            advance(p, limit, False)
            return c

        def counted(p, c):
            advance(p, limit, True)
            return c

        lax.fori_loop(REACH * s, sz.halo, quiet, 0)
        lax.fori_loop(sz.halo, sz.halo + CA, counted, 0)
        lax.fori_loop(sz.halo + CA, last - REACH * s, quiet, 0)
        return limit * (2.0**-12)

    fa[...] = jnp.zeros_like(fa)
    fz[...] = jnp.zeros_like(fz)
    lax.fori_loop(0, sz.sections, step, jnp.float32(1.0))

    def joined(plane):
        return jnp.where(lane < CZ // 2, roll(plane[0:NR], -32), roll(plane[NR:PAIR], 32))

    for c in range(3):
        for a in range(CA):
            out_d[c, a] = joined(fld[c, sz.halo + a])
            out_v[c, a] = joined(fld[3 + c, sz.halo + a])
    pooled = jnp.concatenate(
        [joined(energy[2 * b] + energy[2 * b + 1]) for b in range(CA // 2)], axis=0
    ) * (0.25 / sz.sections)
    rows = out_e.shape[0]
    row_id = lax.broadcasted_iota(jnp.int32, (rows, sz.tab_rows), 0)
    hot = (row_id == wanted[0:1, 0 : sz.tab_rows]).astype(F32)
    out_e[...] = jnp.dot(hot, pooled, precision=NEXACT, preferred_element_type=F32)


def call(body, out_shape, scratch=(), smem_first=False, n_in=0):
    spec = [pl.BlockSpec(memory_space=pltpu.VMEM)] * n_in
    if smem_first:
        spec[0] = pl.BlockSpec(memory_space=pltpu.SMEM)
    return pl.pallas_call(
        body,
        out_shape=[jax.ShapeDtypeStruct(s, F32) for s in out_shape],
        in_specs=spec,
        out_specs=[pl.BlockSpec(memory_space=pltpu.VMEM)] * len(out_shape),
        scratch_shapes=list(scratch),
        compiler_params=pltpu.CompilerParams(vmem_limit_bytes=58 << 20),
    )


def on_device(displace, velocity, stiff, thermal, owner_of, row_of, breaks):
    sz = Sizes(breaks.shape[0])
    groups = lax.axis_size("axial")
    around = lax.axis_size("azim")
    held = thermal.shape[0]
    codes = breaks.reshape(sz.code_rows, CZ)
    wanted = (owner_of.reshape(-1) * held + row_of.reshape(-1)).reshape(CA // 2, NR // 2, 1)
    wanted = jnp.broadcast_to(wanted, (CA // 2, NR // 2, 2)).reshape(sz.tab_rows)
    table = jnp.broadcast_to(wanted[:, None], (sz.tab_rows, CZ))
    lanes = jnp.pad(wanted, (0, CZ - sz.tab_rows))[None, :]

    def body(f):
        return lambda *refs: f(sz, *refs)

    edge = (sz.edge_rows, CZ)
    up, down = call(body(pack_axial), [edge, edge], n_in=5)(displace, velocity, stiff, codes, table)
    low = lax.ppermute(up, "axial", [(i, i + 1) for i in range(groups - 1)])
    high = lax.ppermute(down, "axial", [(i + 1, i) for i in range(groups - 1)])
    everyone = lax.all_gather(thermal, "axial", tiled=True)
    strip = (sz.strip_rows, CZ)
    left, right, temp = call(
        body(pack_azimuth), [strip, strip, (sz.ext // 2 * NR, CZ)], n_in=8
    )(displace, velocity, stiff, codes, table, low, high, everyone)
    strip_r = lax.ppermute(left, "azim", [(i, (i - 1) % around) for i in range(around)])
    strip_l = lax.ppermute(right, "azim", [(i, (i + 1) % around) for i in range(around)])
    first = (lax.axis_index("axial") * CA - sz.halo).astype(jnp.int32).reshape(1)
    plane = (PAIR, CZ)
    n = sz.code_rows * CZ
    scratch = [
        pltpu.VMEM((NFIELD + 1, sz.ext) + plane, F32),
        pltpu.VMEM((NBOND, sz.ext) + plane, F32),
        pltpu.VMEM((NBOND, sz.ext) + plane, F32),
        pltpu.VMEM((NBOND, sz.ext) + plane, F32),
        pltpu.VMEM((sz.ext,) + plane, F32),
        pltpu.VMEM((sz.ext,) + plane, F32),
        pltpu.VMEM((CA,) + plane, F32),
        pltpu.VMEM((NBOND * 4 * NR, n), jnp.bfloat16),
        pltpu.VMEM((4 * CZ, n), jnp.bfloat16),
        pltpu.VMEM((NBOND * 4 * NR, 4 * CZ), F32),
        pltpu.VMEM((NBOND * 16, CA * SLOT), F32),
        pltpu.VMEM((NBOND * 16, CA * SLOT), F32),
    ]
    total = groups * CA
    out_d, out_v, out_e = call(
        lambda *refs: march(sz, total, *refs),
        [displace.shape, velocity.shape, (groups * held, CZ)],
        scratch,
        smem_first=True,
        n_in=11,
    )(first, displace, velocity, stiff, low, high, temp, strip_l, strip_r, codes, lanes)
    parts = out_e.reshape(groups, held, CZ)
    arrived = lax.all_to_all(parts, "axial", split_axis=0, concat_axis=0, tiled=True)
    return out_d, out_v, jnp.sum(arrived, axis=0)


def solution(mesh):
    return jax.shard_map(
        on_device,
        mesh=mesh,
        in_specs=(
            P(None, "axial", None, "azim"),
            P(None, "axial", None, "azim"),
            P("axial", None, "azim"),
            P("axial", "azim"),
            P("axial", "azim", None, None),
            P("axial", "azim", None),
            P(None, "axial", "azim", None),
        ),
        out_specs=(
            P(None, "axial", None, "azim"),
            P(None, "axial", None, "azim"),
            P("axial", "azim"),
        ),
        check_vma=False,
    )
```

```python
import math

import jax
import jax.numpy as jnp
from jax import lax
from jax.experimental import pallas as pl
from jax.experimental.pallas import tpu as pltpu
from jax.sharding import PartitionSpec as P

DILATION = 0.25
DT = 0.2
CA, NR, CZ = 16, 12, 128
REACH = 3
SLOT = 16
PAIR = 2 * NR
PAD = 16
PER = CZ // SLOT
UNROLL = 3
NFIELD = 7
NEXACT = lax.Precision.HIGHEST
F32 = jnp.float32


def offset_table():
    table = []
    for da in range(REACH + 1):
        for dz in range(-REACH, REACH + 1):
            if da * da + dz * dz <= REACH * REACH and (da > 0 or dz > 0):
                table.append((da, 0, dz))
    table.append((0, 1, 0))
    return table


OFFSETS = offset_table()
NBOND = len(OFFSETS)
NUMBER = {o: i for i, o in enumerate(OFFSETS)}


def scales(o):
    return sum(x * x for x in o), math.gcd(math.gcd(o[0], o[1]), abs(o[2]))


def roll(x, shift, axis=1):
    shift %= x.shape[axis]
    return pltpu.roll(x, shift, axis) if shift else x


def lanes_of(shape=(NR, CZ)):
    return lax.broadcasted_iota(jnp.int32, shape, 1)


def dot_nt(a, b):
    return lax.dot_general(a, b, (((1,), (1,)), ((), ())), preferred_element_type=F32)


class Sizes:
    def __init__(self, sections):
        self.sections = sections
        self.halo = REACH * sections
        self.ext = CA + 2 * self.halo
        self.code_rows = 4 * sections
        self.edge_at = {}
        at = PAD
        for f in range(NFIELD):
            for e in range(self.halo):
                if not self.moving(f) or e < self.halo - REACH:
                    self.edge_at[f, e] = at
                    at += NR
        self.tab_at = -(-at // 8) * 8
        self.edge_rows = self.tab_at + PAD
        self.own_tiles = CA // PER
        self.side_rows = PAD + NFIELD * self.own_tiles * NR + PAD
        self.side_rows = -(-self.side_rows // 8) * 8
        self.far_tiles = 2 * self.halo // PER
        self.far_pad = 2 * self.code_rows
        self.heat_tiles = -(-self.ext // 2 // PER)
        self.far_rows = self.far_pad + (NFIELD * self.far_tiles + self.heat_tiles) * NR + PAD
        self.far_rows = -(-self.far_rows // 8) * 8
        self.temp_rows = PAD + self.ext // 2 * NR + PAD

    def moving(self, f):
        return 3 <= f < 6

    def edge_row(self, f, p):
        e = p if p < self.halo else p - self.halo - CA
        if self.moving(f) and p < self.halo:
            e -= REACH
        return self.edge_at.get((f, e))

    def source(self, p):
        if p < self.halo:
            return 0, CA - self.halo + p
        if p < self.halo + CA:
            return 1, p - self.halo
        return 2, p - self.halo - CA

    def side_row(self, f, t):
        return PAD + (f * self.own_tiles + t) * NR

    def far_row(self, f, t):
        return self.far_pad + (f * self.far_tiles + t) * NR


def own_plane(refs, f, a):
    disp, velo, stiff = refs
    ref, g = (disp, f) if f < 3 else (velo, f - 3) if f < 6 else (stiff, 0)
    return ref[pl.ds(g * CA * NR + a, NR, stride=CA), :]


def is_top():
    return lax.broadcasted_iota(jnp.int32, (PAIR, CZ), 0) < NR


def twice(upper, lower, at):
    return jnp.where(is_top(), upper[pl.ds(at, PAIR), :], lower[pl.ds(at - NR, PAIR), :])


def wanted_rows(table, count):
    rows = lax.broadcasted_iota(jnp.int32, (count, table.shape[1]), 0)
    return (rows == table).astype(F32)


def layers_of():
    shape = (CA // 2 * NR, CA // 2 * NR // 2)
    i = lax.broadcasted_iota(jnp.int32, shape, 0)
    j = lax.broadcasted_iota(jnp.int32, shape, 1)
    return (i // 2 == j).astype(F32)


def exact_dot(a, b, dims=((1,), (0,))):
    return lax.dot_general(a, b, (dims, ((), ())), precision=NEXACT, preferred_element_type=F32)


def pack_tiles(sz, planes, left, right, row):
    lane = lanes_of()
    to_left = to_right = None
    for s, x in enumerate(planes):
        if x is None:
            continue
        x = roll(x, SLOT * (s + 1))
        if to_left is None:
            to_left = to_right = x
            continue
        to_right = jnp.where(lane >= SLOT * s, x, to_right)
        n = (s + 1) % PER
        to_left = jnp.where((lane >= SLOT * n) & (lane < SLOT * (n + 1)), x, to_left)
    left[pl.ds(row, NR), :] = to_left
    right[pl.ds(row, NR), :] = to_right


def pack_first(sz, held, disp, velo, stiff, codes, owner, row_of, up, down, left, right, code_f):
    refs = (disp, velo, stiff)
    for f in range(NFIELD):
        for p in range(sz.halo):
            at = sz.edge_row(f, p)
            if at is not None:
                up[pl.ds(at, NR), :] = own_plane(refs, f, CA - sz.halo + p)
            at = sz.edge_row(f, p + sz.halo + CA)
            if at is not None:
                down[pl.ds(at, NR), :] = own_plane(refs, f, p)
        for t in range(sz.own_tiles):
            planes = [own_plane(refs, f, t * PER + s) for s in range(PER)]
            pack_tiles(sz, planes, left, right, sz.side_row(f, t))
    c = codes[...].astype(F32)
    code_f[...] = c
    table = (owner[...] * held + row_of[...]).astype(F32)
    blank = jnp.zeros((PAD, CZ), F32)
    for out in (up, down, left, right):
        out[pl.ds(out.shape[0] - PAD, PAD), :] = blank
        out[pl.ds(0, sz.code_rows), :] = c
    for out in (up, down):
        out[pl.ds(sz.tab_at, 1), pl.ds(0, table.shape[1])] = table


def pack_second(sz, held, low, high, thermal, owner, row_of, left, right, temp):
    n = owner.shape[1]
    rows = thermal.shape[0]
    heat = thermal[...]
    expand = layers_of()
    blank = jnp.zeros((PAD, CZ), F32)
    temp[pl.ds(0, PAD), :] = blank
    temp[pl.ds(sz.temp_rows - PAD, PAD), :] = blank
    at = PAD
    for which in range(3):
        if which == 1:
            table = owner[...] * held + row_of[...]
        else:
            src = low if which == 0 else high
            table = src[pl.ds(sz.tab_at, 1), :][:, 0:n].astype(jnp.int32)
        got = exact_dot(wanted_rows(table, rows), heat, ((0,), (0,)))
        got = exact_dot(expand, got)
        first = (CA - sz.halo) // 2 * NR if which == 0 else 0
        count = (CA if which == 1 else sz.halo) // 2 * NR
        temp[pl.ds(at, count), :] = got[first : first + count]
        at += count
    far = list(range(sz.halo)) + list(range(sz.halo + CA, sz.ext))
    for f in range(NFIELD):
        for t in range(sz.far_tiles):
            planes = []
            for p in far[t * PER : (t + 1) * PER]:
                at = sz.edge_row(f, p)
                src = low if p < sz.halo else high
                planes.append(None if at is None else src[pl.ds(at, NR), :])
            pack_tiles(sz, planes, left, right, sz.far_row(f, t))
    pairs = sz.ext // 2
    for t in range(sz.heat_tiles):
        planes = [temp[pl.ds(PAD + b * NR, NR), :] for b in range(t * PER, min(pairs, (t + 1) * PER))]
        pack_tiles(sz, planes, left, right, sz.far_row(NFIELD, t))
    for out in (left, right):
        out[pl.ds(sz.far_rows - PAD, PAD), :] = blank
        out[pl.ds(0, sz.code_rows), :] = low[pl.ds(0, sz.code_rows), :]
        out[pl.ds(sz.code_rows, sz.code_rows), :] = high[pl.ds(0, sz.code_rows), :]


def decode(codes):
    hi = jnp.floor(codes * (1.0 / CZ))
    z = codes - hi * CZ
    k = jnp.floor((hi + 0.5) * (1.0 / (CA * NR)))
    rest = hi - k * (CA * NR)
    a = jnp.floor((rest + 0.5) * (1.0 / NR))
    return k, a, rest - a * NR, z


def spread(ref, index, rows, chunk, lane_at=0, weigh=False):
    for first in range(0, rows, chunk):
        size = min(chunk, rows - first)
        near = jnp.clip(index - first, -1.0, 256.0)
        at = lax.broadcasted_iota(jnp.int32, (size, CZ), 0).astype(F32).astype(jnp.bfloat16)
        for i in range(index.shape[0]):
            w = jnp.full((size, CZ), 2.0 ** (-12 * (i // 4)) if weigh else 1.0, jnp.bfloat16)
            here = jnp.broadcast_to(near[i : i + 1, :], (size, CZ)).astype(jnp.bfloat16)
            ref[pl.ds(first, size), pl.ds(lane_at + i * CZ, CZ)] = jnp.where(
                at == here, w, jnp.zeros_like(w)
            )


def read_breaks(sz, codes, parts, out, rows_ref, cols_ref, acc):
    at = 0
    for src, lo_group, groups, planes in parts:
        k, a, r, z = decode(src)
        group = jnp.floor(a * 0.25)
        per_k = groups * NR
        rows = -(-NBOND * per_k // 16) * 16
        inside = (group >= lo_group) & (group < lo_group + groups)
        index = jnp.where(inside, k * per_k + (group - lo_group) * NR + r, -1.0)
        spread(rows_ref, index, rows, 240)
        spread(cols_ref, (a - 4 * group) * CZ + z, 4 * CZ, CZ * 2, weigh=True)
        acc[pl.ds(PAD, rows), :] = dot_nt(rows_ref[pl.ds(0, rows), :], cols_ref[...])
        for b in range(NBOND):
            for i, plane in enumerate(planes):
                row = PAD + b * per_k + (plane // 4 - lo_group) * NR
                lanes = pl.ds(plane % 4 * CZ, CZ)
                out[b, at + i] = jnp.where(
                    is_top(), acc[pl.ds(row, PAIR), lanes], acc[pl.ds(row - NR, PAIR), lanes]
                )
        at += len(planes)


def breaks_own(sz, codes, out, rows_ref, cols_ref, acc):
    acc[pl.ds(0, PAD), :] = jnp.zeros((PAD, 4 * CZ), F32)
    parts = [(codes[...], 0, CA // 4, list(range(CA)))]
    read_breaks(sz, None, parts, out, rows_ref, cols_ref, acc)


def breaks_far(sz, low, high, out, rows_ref, cols_ref, acc):
    acc[pl.ds(0, PAD), :] = jnp.zeros((PAD, 4 * CZ), F32)
    n = sz.code_rows
    parts = [
        (low[pl.ds(0, n), :], (CA - sz.halo) // 4, sz.halo // 4, list(range(CA - sz.halo, CA))),
        (high[pl.ds(0, n), :], 0, sz.halo // 4, list(range(sz.halo))),
    ]
    read_breaks(sz, None, parts, out, rows_ref, cols_ref, acc)


def side_breaks(sz, sources, broken, rows_ref, cols_ref, acc, edge):
    n = sz.code_rows * CZ
    rows = -(-NBOND * PAIR // 16) * 16
    for which, (left, right) in enumerate(sources):
        k, a, r, z = decode(left)
        spread(rows_ref, k * PAIR + r, rows, 240)
        spread(cols_ref, jnp.where(z >= CZ - SLOT, a * SLOT + z - (CZ - SLOT), -1.0), CA * SLOT, 256, weigh=True)
        k, a, r, z = decode(right)
        spread(rows_ref, k * PAIR + NR + r, rows, 240, lane_at=n)
        tile = jnp.floor(a * (1.0 / PER))
        slot = a - tile * PER + 1
        slot = jnp.where(slot == PER, 0.0, slot)
        spread(cols_ref, jnp.where(z < SLOT, tile * CZ + slot * SLOT + z, -1.0), CA * SLOT, 256, n, weigh=True)
        acc[...] = dot_nt(rows_ref[...], cols_ref[...])
        for p in range(sz.ext):
            if sz.source(p)[0] != which:
                continue
            a = sz.source(p)[1]
            for b in range(NBOND):
                x = acc[pl.ds(b * PAIR, PAIR), pl.ds(a // PER * CZ, CZ)]
                broken[b, p] = jnp.where(edge, roll(x, SLOT * (PER - 1 - a % PER)), broken[b, p])


def march(
    sz, total, held, first, disp, velo, stiff, low, high, temp, side_l, side_r, far_l, far_r, codes, owner, row_of,
    w_own, w_far, out_d, out_v, out_e, fld, stiffk, heatk, broken, fa, fz, energy, pooled, rows_ref, cols_ref, acc, sems,
):
    refs = (disp, velo, stiff)
    halo = sz.halo
    moves = [
        pltpu.make_async_copy(w_own, broken.at[:, pl.ds(halo, CA)], sems.at[0]),
        pltpu.make_async_copy(w_far.at[:, pl.ds(0, halo)], broken.at[:, pl.ds(0, halo)], sems.at[1]),
        pltpu.make_async_copy(w_far.at[:, pl.ds(halo, halo)], broken.at[:, pl.ds(halo + CA, halo)], sems.at[2]),
    ]
    for m in moves:
        m.start()
    lane = lanes_of()
    wide = lanes_of((PAIR, CZ))
    top = is_top()
    edge = (top & (wide >= CZ - SLOT)) | (~top & (wide < SLOT))
    n = sz.code_rows
    for f in range(NFIELD + 1):
        for p in range(sz.ext):
            which, a = sz.source(p)
            if f == NFIELD:
                x = twice(temp, temp, PAD + p // 2 * NR)
                s = p // 2
                t, s = s // PER, s % PER
                y = twice(far_l, far_r, sz.far_row(NFIELD, t))
            elif which == 1:
                x = own_plane(refs, f, a)
                x = jnp.concatenate([x, x], axis=0)
                t, s = a // PER, a % PER
                y = twice(side_l, side_r, sz.side_row(f, t))
            else:
                at = sz.edge_row(f, p)
                if at is None:
                    continue
                src = low if which == 0 else high
                x = twice(src, src, at)
                q = p if which == 0 else p - CA
                t, s = q // PER, q % PER
                y = twice(far_l, far_r, sz.far_row(f, t))
            fld[f, p] = jnp.where(edge, roll(y, SLOT * (PER - 1 - s)), x)

    row = lax.broadcasted_iota(jnp.int32, (PAIR, CZ), 0)
    not_top = jnp.where((row == NR - 1) | (row == PAIR - 1), 0.0, 1.0)
    start = first[0]

    def prepare(p):
        at = start + p
        live = [
            jnp.where((at >= 0) & (at + da < total), 1.0, 0.0).astype(F32) for da in range(REACH + 1)
        ]
        for k, (da, dr, dz) in enumerate(OFFSETS):
            n2, d = scales((da, dr, dz))
            c = fld[6, p]
            h = fld[7, p]
            if dr:
                c2, h2 = roll(c, -1, 0), roll(h, -1, 0)
            else:
                c2, h2 = roll(fld[6, p + da], -dz), roll(fld[7, p + da], -dz)
            m = (c + c2) * (live[da] * (0.5 * d * d / (n2 * n2)))
            stiffk[k, p] = m * not_top if dr else m
            heatk[k, p] = (h + h2) * (DILATION * 0.5 * n2 / d)

    def several(body, count):
        def run(first_plane, times):
            def one(i, c):
                for j in range(count):
                    body(first_plane + i * count + j)
                return c

            lax.fori_loop(0, times, one, 0)

        return run

    several(prepare, UNROLL)(0, (sz.ext - 1) // UNROLL)
    for m in moves:
        m.wait()
    side_breaks(
        sz,
        [
            (far_l[pl.ds(0, n), :], far_r[pl.ds(0, n), :]),
            (side_l[pl.ds(0, n), :], side_r[pl.ds(0, n), :]),
            (far_l[pl.ds(n, n), :], far_r[pl.ds(n, n), :]),
        ],
        broken, rows_ref, cols_ref, acc, edge,
    )
    energy[...] = jnp.zeros_like(energy)

    def advance(p, limit, with_energy):
        ua, ur, uz = fld[0, p], fld[1, p], fld[2, p]
        sums = {}

        def bond(o, elongation):
            k = NUMBER[o]
            q = elongation - heatk[k, p]
            g = jnp.where(broken[k, p] >= limit, 0.0, stiffk[k, p]) * q
            if with_energy:
                n2 = scales(o)[0]
                sums[n2] = sums[n2] + g * q if n2 in sums else g * q
            return g

        force_a = fa[p]
        force_z = fz[p]
        for dz in (1, 2, 3):
            g = bond((0, 0, dz), roll(uz, -dz) - uz)
            force_z = force_z + (g - roll(g, dz))
        g = bond((0, 1, 0), roll(ur, -1, 0) - ur)
        force_r = g - roll(g, 1, 0)
        for da in (1, 2):
            ua2, uz2 = fld[0, p + da], fld[2, p + da]
            g = bond((da, 0, 0), ua2 - ua)
            force_a = force_a + g
            push_a = g
            push_z = None
            for dz in (1, 2):
                gs = []
                for sign in (1, -1):
                    dua = roll(ua2, -sign * dz) - ua
                    duz = roll(uz2, -sign * dz) - uz
                    if da == dz:
                        e = dua + duz if sign > 0 else dua - duz
                    elif dz == 2:
                        e = dua + (2.0 * sign) * duz
                    else:
                        e = 2.0 * dua + duz if sign > 0 else 2.0 * dua - duz
                    gs.append(bond((da, 0, sign * dz), e))
                ma = 1.0 if da == dz else float(da)
                mz = 1.0 if da == dz else float(dz)
                own_s, own_d = gs[0] + gs[1], gs[0] - gs[1]
                plus, minus = roll(gs[0], dz), roll(gs[1], -dz)
                far_s, far_d = plus + minus, plus - minus
                if ma != 1.0:
                    own_s, far_s = ma * own_s, ma * far_s
                if mz != 1.0:
                    own_d, far_d = mz * own_d, mz * far_d
                force_a = force_a + own_s
                force_z = force_z + own_d
                push_a = push_a + far_s
                push_z = far_d if push_z is None else push_z + far_d
            fa[p + da] = fa[p + da] - push_a
            fz[p + da] = fz[p + da] - push_z
        g = bond((3, 0, 0), fld[0, p + 3] - ua)
        force_a = force_a + g
        fa[p + 3] = -g
        fz[p + 3] = jnp.zeros_like(g)
        for f, u, force in ((0, ua, force_a), (1, ur, force_r), (2, uz, force_z)):
            v = fld[3 + f, p] + DT * force
            fld[3 + f, p] = v
            fld[f, p] = u + DT * v
        if with_energy:
            e = None
            for n2, x in sums.items():
                y = x * (0.5 / math.sqrt(n2))
                e = y if e is None else e + y
            energy[p - sz.halo] = energy[p - sz.halo] + e

    counted = -(-CA // UNROLL)

    def step(s, limit):
        quiet = several(lambda p: advance(p, limit, False), UNROLL)
        quiet(REACH * s, sz.sections - s)
        several(lambda p: advance(p, limit, True), UNROLL)(halo, counted)
        quiet(halo + counted * UNROLL, sz.sections - 1 - s)
        return limit * (2.0**-12)

    fa[...] = jnp.zeros_like(fa)
    fz[...] = jnp.zeros_like(fz)
    lax.fori_loop(0, sz.sections, step, jnp.float32(1.0))

    half = lane < CZ // 2
    for c in range(3):
        for a in range(CA):
            at = pl.ds(c * CA * NR + a, NR, stride=CA)
            p = halo + a
            out_d[at, :] = jnp.where(half, fld[c, p, pl.ds(0, NR), :], fld[c, p, pl.ds(NR, NR), :])
            out_v[at, :] = jnp.where(half, fld[3 + c, p, pl.ds(0, NR), :], fld[3 + c, p, pl.ds(NR, NR), :])
    for b in range(CA // 2):
        up = energy[2 * b, pl.ds(0, NR), :] + energy[2 * b + 1, pl.ds(0, NR), :]
        dn = energy[2 * b, pl.ds(NR, NR), :] + energy[2 * b + 1, pl.ds(NR, NR), :]
        pooled[pl.ds(b * NR, NR), :] = jnp.where(half, up, dn) * (0.25 / sz.sections)
    mean = exact_dot(layers_of(), pooled[...], ((0,), (0,)))
    table = owner[...] * held + row_of[...]
    out_e[...] = exact_dot(wanted_rows(table, out_e.shape[0]), mean)


def call(body, ins, outs, scratch=(), name=None):
    arrays = [i[0] if isinstance(i, tuple) else i for i in ins]
    spaces = [i[1] if isinstance(i, tuple) else pltpu.VMEM for i in ins]
    scratch = list(scratch)
    size = sum(math.prod(s.shape) * s.dtype.itemsize for s in scratch if hasattr(s, "shape") and s.dtype in (F32, jnp.bfloat16))
    size += sum(4 * math.prod(s) for s in outs)
    size += sum(4 * math.prod(a.shape) for a, m in zip(arrays, spaces) if m is pltpu.VMEM)
    return pl.pallas_call(
        body,
        name=name,
        out_shape=[jax.ShapeDtypeStruct(s, F32) for s in outs],
        in_specs=[pl.BlockSpec(memory_space=m) for m in spaces],
        out_specs=[pl.BlockSpec(memory_space=pltpu.VMEM)] * len(outs),
        scratch_shapes=scratch,
        compiler_params=pltpu.CompilerParams(vmem_limit_bytes=min(60 << 20, size + (6 << 20))),
    )(*arrays)


def on_device(displace, velocity, stiff, thermal, owner_of, row_of, breaks):
    sz = Sizes(breaks.shape[0])
    groups = lax.axis_size("axial")
    around = lax.axis_size("azim")
    held = thermal.shape[0]
    nreq = row_of.shape[-1]
    codes = breaks.reshape(sz.code_rows, CZ)
    owner = owner_of.reshape(1, nreq)
    local = row_of.reshape(1, nreq)
    disp = displace.transpose(0, 2, 1, 3).reshape(3 * NR * CA, CZ)
    velo = velocity.transpose(0, 2, 1, 3).reshape(3 * NR * CA, CZ)
    stif = stiff.transpose(1, 0, 2).reshape(NR * CA, CZ)

    edge, side, far = (sz.edge_rows, CZ), (sz.side_rows, CZ), (sz.far_rows, CZ)
    up, down, left, right, code_f = call(
        lambda *refs: pack_first(sz, held, *refs),
        [disp, velo, stif, codes, owner, local],
        [edge, edge, side, side, (sz.code_rows, CZ)],
        name="pack_first",
    )
    to_left = [(i, (i - 1) % around) for i in range(around)]
    to_right = [(i, (i + 1) % around) for i in range(around)]
    low = lax.ppermute(up, "axial", [(i, i + 1) for i in range(groups - 1)])
    high = lax.ppermute(down, "axial", [(i + 1, i) for i in range(groups - 1)])
    side_r = lax.ppermute(left, "azim", to_left)
    side_l = lax.ppermute(right, "azim", to_right)
    spread_heat = jnp.broadcast_to(thermal[None], (groups,) + thermal.shape)
    everyone = lax.all_to_all(spread_heat, "axial", split_axis=0, concat_axis=0, tiled=True)
    everyone = everyone.reshape(groups * held, CZ)

    plane = (PAIR, CZ)
    n = sz.code_rows * CZ
    tall = NBOND * CA // 4 * NR
    work = [
        pltpu.VMEM((tall, n), jnp.bfloat16),
        pltpu.VMEM((4 * CZ, n), jnp.bfloat16),
        pltpu.VMEM((tall + 2 * PAD, 4 * CZ), F32),
    ]
    (w_own,) = call(
        lambda *refs: breaks_own(sz, *refs), [code_f], [(NBOND, CA) + plane], work, name="breaks_own"
    )
    left, right, temp = call(
        lambda *refs: pack_second(sz, held, *refs),
        [low, high, everyone, owner, local],
        [far, far, (sz.temp_rows, CZ)],
        name="pack_second",
    )
    far_r = lax.ppermute(left, "azim", to_left)
    far_l = lax.ppermute(right, "azim", to_right)
    (w_far,) = call(
        lambda *refs: breaks_far(sz, *refs), [low, high], [(NBOND, 2 * sz.halo) + plane], work, name="breaks_far"
    )
    first = (lax.axis_index("axial") * CA - sz.halo).astype(jnp.int32).reshape(1)
    planes = sz.ext + 2
    strip = -(-NBOND * PAIR // 16) * 16
    scratch = [
        pltpu.VMEM((NFIELD + 1, planes) + plane, F32),
        pltpu.VMEM((NBOND, sz.ext) + plane, F32),
        pltpu.VMEM((NBOND, sz.ext) + plane, F32),
        pltpu.VMEM((NBOND, sz.ext) + plane, F32),
        pltpu.VMEM((planes,) + plane, F32),
        pltpu.VMEM((planes,) + plane, F32),
        pltpu.VMEM((-(-CA // UNROLL) * UNROLL,) + plane, F32),
        pltpu.VMEM((CA // 2 * NR, CZ), F32),
        pltpu.VMEM((strip, 2 * n), jnp.bfloat16),
        pltpu.VMEM((CA * SLOT, 2 * n), jnp.bfloat16),
        pltpu.VMEM((strip, CA * SLOT), F32),
        pltpu.SemaphoreType.DMA((3,)),
    ]
    total = groups * CA
    out_d, out_v, out_e = call(
        lambda *refs: march(sz, total, held, *refs),
        [
            (first, pltpu.SMEM), disp, velo, stif, low, high, temp, side_l, side_r, far_l, far_r, code_f, owner, local,
            (w_own, pl.ANY), (w_far, pl.ANY),
        ],
        [disp.shape, velo.shape, (groups * held, CZ)],
        scratch,
        name="march",
    )
    parts = out_e.reshape(groups, held, CZ)
    arrived = lax.all_to_all(parts, "axial", split_axis=0, concat_axis=0, tiled=True)
    shape = (3, NR, CA, CZ)
    return (
        out_d.reshape(shape).transpose(0, 2, 1, 3),
        out_v.reshape(shape).transpose(0, 2, 1, 3),
        jnp.sum(arrived, axis=0),
    )


def solution(mesh):
    return jax.shard_map(
        on_device,
        mesh=mesh,
        in_specs=(
            P(None, "axial", None, "azim"),
            P(None, "axial", None, "azim"),
            P("axial", None, "azim"),
            P("axial", "azim"),
            P("axial", "azim", None, None),
            P("axial", "azim", None),
            P(None, "axial", "azim", None),
        ),
        out_specs=(
            P(None, "axial", None, "azim"),
            P(None, "axial", None, "azim"),
            P("axial", "azim"),
        ),
        check_vma=False,
    )
```

```python
import math

import jax
import jax.numpy as jnp
from jax import lax
from jax.experimental import pallas as pl
from jax.experimental.pallas import tpu as pltpu
from jax.sharding import PartitionSpec as P

DILATION = 0.25
DT = 0.2
CA, NR, CZ = 16, 12, 128
REACH = 3
SLOT = 16
PAIR = 2 * NR
PAD = 16
PER = CZ // SLOT
UNROLL = 3
NFIELD = 7
NEXACT = lax.Precision.HIGHEST
F32 = jnp.float32


def offset_table():
    table = []
    for da in range(REACH + 1):
        for dz in range(-REACH, REACH + 1):
            if da * da + dz * dz <= REACH * REACH and (da > 0 or dz > 0):
                table.append((da, 0, dz))
    table.append((0, 1, 0))
    return table


OFFSETS = offset_table()
NBOND = len(OFFSETS)
NUMBER = {o: i for i, o in enumerate(OFFSETS)}


def scales(o):
    return sum(x * x for x in o), math.gcd(math.gcd(o[0], o[1]), abs(o[2]))


def roll(x, shift, axis=1):
    shift %= x.shape[axis]
    return pltpu.roll(x, shift, axis) if shift else x


def lanes_of(shape=(NR, CZ)):
    return lax.broadcasted_iota(jnp.int32, shape, 1)


def dot_nt(a, b):
    return lax.dot_general(a, b, (((1,), (1,)), ((), ())), preferred_element_type=F32)


class Sizes:
    def __init__(self, sections):
        self.sections = sections
        self.halo = REACH * sections
        self.ext = CA + 2 * self.halo
        self.code_rows = 4 * sections
        self.edge_at = {}
        at = PAD
        for f in range(NFIELD):
            for e in range(self.halo):
                if not self.moving(f) or e < self.halo - REACH:
                    self.edge_at[f, e] = at
                    at += NR
        self.tab_at = -(-at // 8) * 8
        self.edge_rows = self.tab_at + PAD
        self.own_tiles = CA // PER
        self.side_rows = PAD + NFIELD * self.own_tiles * NR + PAD
        self.side_rows = -(-self.side_rows // 8) * 8
        self.far_tiles = 2 * self.halo // PER
        self.far_pad = PAD
        self.heat_tiles = -(-self.ext // 2 // PER)
        self.far_rows = self.far_pad + (NFIELD * self.far_tiles + self.heat_tiles) * NR + PAD
        self.far_rows = -(-self.far_rows // 8) * 8
        self.temp_rows = PAD + self.ext // 2 * NR + PAD

    def moving(self, f):
        return 3 <= f < 6

    def edge_row(self, f, p):
        e = p if p < self.halo else p - self.halo - CA
        if self.moving(f) and p < self.halo:
            e -= REACH
        return self.edge_at.get((f, e))

    def source(self, p):
        if p < self.halo:
            return 0, CA - self.halo + p
        if p < self.halo + CA:
            return 1, p - self.halo
        return 2, p - self.halo - CA

    def side_row(self, f, t):
        return PAD + (f * self.own_tiles + t) * NR

    def far_row(self, f, t):
        return self.far_pad + (f * self.far_tiles + t) * NR


def own_plane(refs, f, a):
    disp, velo, stiff = refs
    ref, g = (disp, f) if f < 3 else (velo, f - 3) if f < 6 else (stiff, 0)
    return ref[pl.ds(g * CA * NR + a, NR, stride=CA), :]


def is_top():
    return lax.broadcasted_iota(jnp.int32, (PAIR, CZ), 0) < NR


def twice(upper, lower, at):
    return jnp.where(is_top(), upper[pl.ds(at, PAIR), :], lower[pl.ds(at - NR, PAIR), :])


def wanted_rows(table, count):
    rows = lax.broadcasted_iota(jnp.int32, (count, table.shape[1]), 0)
    return (rows == table).astype(F32)


def layers_of():
    shape = (CA // 2 * NR, CA // 2 * NR // 2)
    i = lax.broadcasted_iota(jnp.int32, shape, 0)
    j = lax.broadcasted_iota(jnp.int32, shape, 1)
    return (i // 2 == j).astype(F32)


def exact_dot(a, b, dims=((1,), (0,))):
    return lax.dot_general(a, b, (dims, ((), ())), precision=NEXACT, preferred_element_type=F32)


def pack_tiles(sz, planes, left, right, row):
    lane = lanes_of()
    to_left = to_right = None
    for s, x in enumerate(planes):
        if x is None:
            continue
        x = roll(x, SLOT * (s + 1))
        if to_left is None:
            to_left = to_right = x
            continue
        to_right = jnp.where(lane >= SLOT * s, x, to_right)
        n = (s + 1) % PER
        to_left = jnp.where((lane >= SLOT * n) & (lane < SLOT * (n + 1)), x, to_left)
    left[pl.ds(row, NR), :] = to_left
    right[pl.ds(row, NR), :] = to_right


def pack_first(sz, share, disp, velo, stiff, codes, owner, row_of, up, down, left, right, code_f):
    refs = (disp, velo, stiff)
    for f in range(NFIELD):
        for p in range(sz.halo):
            at = sz.edge_row(f, p)
            if at is not None:
                up[pl.ds(at, NR), :] = own_plane(refs, f, CA - sz.halo + p)
            at = sz.edge_row(f, p + sz.halo + CA)
            if at is not None:
                down[pl.ds(at, NR), :] = own_plane(refs, f, p)
        for t in range(sz.own_tiles):
            planes = [own_plane(refs, f, t * PER + s) for s in range(PER)]
            pack_tiles(sz, planes, left, right, sz.side_row(f, t))
    c = codes[...].astype(F32)
    code_f[...] = c
    table = (owner[...] * share + row_of[...]).astype(F32)
    blank = jnp.zeros((PAD, CZ), F32)
    for out in (up, down, left, right):
        out[pl.ds(out.shape[0] - PAD, PAD), :] = blank
        out[pl.ds(0, sz.code_rows), :] = c
    for out in (up, down):
        out[pl.ds(sz.tab_at, 1), pl.ds(0, table.shape[1])] = table


def pack_second(sz, held, share, low, high, thermal, owner, row_of, left, right, temp):
    n = owner.shape[1]
    rows = thermal.shape[0]
    heat = thermal[...]
    expand = layers_of()
    blank = jnp.zeros((PAD, CZ), F32)
    temp[pl.ds(0, PAD), :] = blank
    temp[pl.ds(sz.temp_rows - PAD, PAD), :] = blank
    at = PAD
    for which in range(3):
        if which == 1:
            table = owner[...] * share + row_of[...]
        else:
            src = low if which == 0 else high
            table = src[pl.ds(sz.tab_at, 1), :][:, 0:n].astype(jnp.int32)
        got = exact_dot(wanted_rows(table, rows), heat, ((0,), (0,)))
        got = exact_dot(expand, got)
        first = (CA - sz.halo) // 2 * NR if which == 0 else 0
        count = (CA if which == 1 else sz.halo) // 2 * NR
        temp[pl.ds(at, count), :] = got[first : first + count]
        at += count
    far = list(range(sz.halo)) + list(range(sz.halo + CA, sz.ext))
    for f in range(NFIELD):
        for t in range(sz.far_tiles):
            planes = []
            for p in far[t * PER : (t + 1) * PER]:
                at = sz.edge_row(f, p)
                src = low if p < sz.halo else high
                planes.append(None if at is None else src[pl.ds(at, NR), :])
            pack_tiles(sz, planes, left, right, sz.far_row(f, t))
    pairs = sz.ext // 2
    for t in range(sz.heat_tiles):
        planes = [temp[pl.ds(PAD + b * NR, NR), :] for b in range(t * PER, min(pairs, (t + 1) * PER))]
        pack_tiles(sz, planes, left, right, sz.far_row(NFIELD, t))
    for out in (left, right):
        out[pl.ds(sz.far_rows - PAD, PAD), :] = blank
        out[pl.ds(0, PAD), :] = blank


def relay(groups, thermal, side_l, side_r, box):
    rows = thermal.shape[0]
    n = side_l.shape[0]
    for g in range(groups):
        at = g * (rows + 2 * n)
        box[pl.ds(at, rows), :] = thermal[...]
        box[pl.ds(at + rows, n), :] = side_l[...]
        box[pl.ds(at + rows + n, n), :] = side_r[...]


def decode(codes):
    hi = jnp.floor(codes * (1.0 / CZ))
    z = codes - hi * CZ
    k = jnp.floor((hi + 0.5) * (1.0 / (CA * NR)))
    rest = hi - k * (CA * NR)
    a = jnp.floor((rest + 0.5) * (1.0 / NR))
    return k, a, rest - a * NR, z


def spread(ref, index, rows, chunk, lane_at=0, weigh=False):
    for first in range(0, rows, chunk):
        size = min(chunk, rows - first)
        near = jnp.clip(index - first, -1.0, 256.0)
        at = lax.broadcasted_iota(jnp.int32, (size, CZ), 0).astype(F32).astype(jnp.bfloat16)
        for i in range(index.shape[0]):
            w = jnp.full((size, CZ), 2.0 ** (-12 * (i // 4)) if weigh else 1.0, jnp.bfloat16)
            here = jnp.broadcast_to(near[i : i + 1, :], (size, CZ)).astype(jnp.bfloat16)
            ref[pl.ds(first, size), pl.ds(lane_at + i * CZ, CZ)] = jnp.where(
                at == here, w, jnp.zeros_like(w)
            )


def read_breaks(sz, parts, out, rows_ref, cols_ref, acc):
    for src, lo_group, groups, first, count, at in parts:
        k, a, r, z = decode(src)
        group = jnp.floor(a * 0.25)
        per_k = groups * NR
        rows = -(-NBOND * per_k // 16) * 16
        inside = (group >= lo_group) & (group < lo_group + groups)
        index = jnp.where(inside, k * per_k + (group - lo_group) * NR + r, -1.0)
        spread(rows_ref, index, rows, 240)
        spread(cols_ref, (a - 4 * group) * CZ + z, 4 * CZ, CZ * 2, weigh=True)
        acc[pl.ds(PAD, rows), :] = dot_nt(rows_ref[pl.ds(0, rows), :], cols_ref[...])
        for b in range(NBOND):
            for i in range(count):
                plane = first + i
                row = PAD + b * per_k + (plane // 4 - lo_group) * NR
                lanes = pl.ds(plane % 4 * CZ, CZ)
                out[b, at + i] = jnp.where(
                    is_top(), acc[pl.ds(row, PAIR), lanes], acc[pl.ds(row - NR, PAIR), lanes]
                )


def breaks_own(sz, codes, out, rows_ref, cols_ref, acc):
    acc[pl.ds(0, PAD), :] = jnp.zeros((PAD, 4 * CZ), F32)
    read_breaks(sz, [(codes[...], 0, CA // 4, 0, CA, 0)], out, rows_ref, cols_ref, acc)


def breaks_all(
    sz, at_lo, at_hi, own, low, high, side_l, side_r, box, out, rows_ref, cols_ref, acc, rows_s, cols_s, acc_s
):
    n, halo = sz.code_rows, sz.halo
    acc[pl.ds(0, PAD), :] = jnp.zeros((PAD, 4 * CZ), F32)
    parts = [
        (low[...], (CA - halo) // 4, halo // 4, CA - halo, halo, 0),
        (high[...], 0, halo // 4, 0, halo, halo + CA),
    ]
    read_breaks(sz, parts, out, rows_ref, cols_ref, acc)
    wide = lanes_of((PAIR, CZ))
    edge = (is_top() & (wide >= CZ - SLOT)) | (~is_top() & (wide < SLOT))
    sources = [
        (box[pl.ds(at_lo, n), :], box[pl.ds(at_lo + n, n), :]),
        (side_l[...], side_r[...]),
        (box[pl.ds(at_hi, n), :], box[pl.ds(at_hi + n, n), :]),
    ]
    side_breaks(sz, sources, own, out, rows_s, cols_s, acc_s, edge)


def side_breaks(sz, sources, own, out, rows_ref, cols_ref, acc, edge):
    n = sz.code_rows * CZ
    rows = -(-NBOND * PAIR // 16) * 16
    for which, (left, right) in enumerate(sources):
        k, a, r, z = decode(left)
        spread(rows_ref, k * PAIR + r, rows, 240)
        spread(cols_ref, jnp.where(z >= CZ - SLOT, a * SLOT + z - (CZ - SLOT), -1.0), CA * SLOT, 256, weigh=True)
        k, a, r, z = decode(right)
        spread(rows_ref, k * PAIR + NR + r, rows, 240, lane_at=n)
        tile = jnp.floor(a * (1.0 / PER))
        slot = a - tile * PER + 1
        slot = jnp.where(slot == PER, 0.0, slot)
        spread(cols_ref, jnp.where(z < SLOT, tile * CZ + slot * SLOT + z, -1.0), CA * SLOT, 256, n, weigh=True)
        acc[...] = dot_nt(rows_ref[...], cols_ref[...])
        for p in range(sz.ext):
            if sz.source(p)[0] != which:
                continue
            a = sz.source(p)[1]
            for b in range(NBOND):
                x = acc[pl.ds(b * PAIR, PAIR), pl.ds(a // PER * CZ, CZ)]
                old = own[b, a] if which == 1 else out[b, p]
                out[b, p] = jnp.where(edge, roll(x, SLOT * (PER - 1 - a % PER)), old)


def march(
    sz, total, held, place, disp, velo, stiff, low, high, temp, side_l, side_r, far_l, far_r, owner, row_of,
    broken, out_d, out_v, out_e, fld, stiffk, heatk, bonds, forces, wait_a, wait_b, energy, pooled,
):
    refs = (disp, velo, stiff)
    halo = sz.halo
    lane = lanes_of()
    wide = lanes_of((PAIR, CZ))
    top = is_top()
    edge = (top & (wide >= CZ - SLOT)) | (~top & (wide < SLOT))
    for f in range(NFIELD + 1):
        for p in range(sz.ext):
            which, a = sz.source(p)
            if f == NFIELD:
                x = twice(temp, temp, PAD + p // 2 * NR)
                s = p // 2
                t, s = s // PER, s % PER
                y = twice(far_l, far_r, sz.far_row(NFIELD, t))
            elif which == 1:
                x = own_plane(refs, f, a)
                x = jnp.concatenate([x, x], axis=0)
                t, s = a // PER, a % PER
                y = twice(side_l, side_r, sz.side_row(f, t))
            else:
                at = sz.edge_row(f, p)
                if at is None:
                    continue
                src = low if which == 0 else high
                x = twice(src, src, at)
                q = p if which == 0 else p - CA
                t, s = q // PER, q % PER
                y = twice(far_l, far_r, sz.far_row(f, t))
            fld[f, p] = jnp.where(edge, roll(y, SLOT * (PER - 1 - s)), x)

    row = lax.broadcasted_iota(jnp.int32, (PAIR, CZ), 0)
    not_top = jnp.where((row == NR - 1) | (row == PAIR - 1), 0.0, 1.0)
    start = place[0] * CA - halo

    def turned(cache, f, p, i, dz):
        key = f, i, dz
        if key not in cache:
            x = turned(cache, f, p, i, 0) if dz else fld[f, p + i]
            cache[key] = roll(x, -dz)
        return cache[key]

    def prepare(p):
        cache = {}
        get = lambda f, i, dz=0: turned(cache, f, p, i, dz)
        for i in range(UNROLL):
            at = start + p + i
            live = [
                jnp.where((at >= 0) & (at + da < total), 1.0, 0.0).astype(F32) for da in range(REACH + 1)
            ]
            c, h = get(6, i), get(7, i)
            for k, (da, dr, dz) in enumerate(OFFSETS):
                n2, d = scales((da, dr, dz))
                if dr:
                    c2, h2 = roll(c, -1, 0), roll(h, -1, 0)
                else:
                    c2, h2 = get(6, i + da, dz), get(7, i + da, dz)
                m = (c + c2) * (live[da] * (0.5 * d * d / (n2 * n2)))
                stiffk[k, p + i] = m * not_top if dr else m
                heatk[k, p + i] = (h + h2) * (DILATION * 0.5 * n2 / d)

    def several(body, first_plane, times):
        def one(i, c):
            body(first_plane + i * UNROLL)
            return c

        lax.fori_loop(0, times, one, 0)

    several(prepare, 0, (sz.ext - 1) // UNROLL)
    energy[...] = jnp.zeros_like(energy)

    span = range(UNROLL)

    def pull(p, limit, with_energy):
        cache = {}
        get = lambda f, i, dz=0: turned(cache, f, p, i, dz)
        fa_at = {i: wait_a[i] for i in range(REACH)}
        fz_at = {}
        sums = [{} for _ in span]
        keep = []

        def add(to, i, x):
            to[i] = to[i] + x if i in to else x

        def bond(i, o, elongation):
            k = NUMBER[o]
            q = elongation - heatk[k, p + i]
            g = jnp.where(broken[k, p + i] >= limit, 0.0, stiffk[k, p + i]) * q
            if with_energy:
                add(sums[i], scales(o)[0], g * q)
            if o[2]:
                keep.append((bonds, (k, i), g))
            return g

        for i in span:
            ua, ur, uz = get(0, i), get(1, i), get(2, i)
            for dz in (1, 2, 3):
                add(fz_at, i, bond(i, (0, 0, dz), get(2, i, dz) - uz))
            g = bond(i, (0, 1, 0), roll(ur, -1, 0) - ur)
            keep.append((forces, (1, i), g - roll(g, 1, 0)))
            for da in (1, 2):
                j = i + da
                g = bond(i, (da, 0, 0), get(0, j) - ua)
                add(fa_at, i, g)
                add(fa_at, j, -g)
                for dz in (1, 2):
                    gs = []
                    for sign in (1, -1):
                        dua = get(0, j, sign * dz) - ua
                        duz = get(2, j, sign * dz) - uz
                        if da == dz:
                            e = dua + duz if sign > 0 else dua - duz
                        elif dz == 2:
                            e = dua + (2.0 * sign) * duz
                        else:
                            e = 2.0 * dua + duz if sign > 0 else 2.0 * dua - duz
                        gs.append(bond(i, (da, 0, sign * dz), e))
                    own_s, own_d = gs[0] + gs[1], gs[0] - gs[1]
                    add(fa_at, i, own_s if da in (1, dz) else float(da) * own_s)
                    add(fz_at, i, own_d if dz in (1, da) else float(dz) * own_d)
            g = bond(i, (3, 0, 0), get(0, i + 3) - ua)
            add(fa_at, i, g)
            add(fa_at, i + 3, -g)
            keep.append((forces, (0, i), fa_at[i]))
            keep.append((forces, (2, i), fz_at[i]))
        keep += [(wait_a, (i,), fa_at[i + UNROLL]) for i in range(REACH)]
        if with_energy:
            for i in span:
                e = None
                for n2, x in sums[i].items():
                    y = x * (0.5 / math.sqrt(n2))
                    e = y if e is None else e + y
                keep.append((energy, (p + i - halo,), energy[p + i - halo] + e))
        return keep

    def push(p):
        fa_at = {i: wait_b[0, i] for i in range(REACH - 1)}
        fz_at = {i: wait_b[1, i] for i in range(REACH - 1)}
        keep = []

        def add(to, i, x):
            to[i] = to[i] + x if i in to else x

        for i in span:
            for da in (0, 1, 2):
                j = i + da
                for dz in (1, 2) if da else (1, 2, 3):
                    plus = roll(bonds[NUMBER[da, 0, dz], i], dz)
                    if da == 0:
                        add(fz_at, j, plus)
                        continue
                    minus = roll(bonds[NUMBER[da, 0, -dz], i], -dz)
                    both, gap = plus + minus, plus - minus
                    add(fa_at, j, both if da in (1, dz) else float(da) * both)
                    add(fz_at, j, gap if dz in (1, da) else float(dz) * gap)
            for f, force in (
                (0, forces[0, i] - fa_at[i]),
                (1, forces[1, i]),
                (2, forces[2, i] - fz_at[i]),
            ):
                v = fld[3 + f, p + i] + DT * force
                keep.append((fld, (3 + f, p + i), v))
                keep.append((fld, (f, p + i), fld[f, p + i] + DT * v))
        for i in range(REACH - 1):
            keep.append((wait_b, (0, i), fa_at[UNROLL + i]))
            keep.append((wait_b, (1, i), fz_at[UNROLL + i]))
        return keep

    def store(keep):
        for ref, index, value in keep:
            ref[index] = value

    def both_halves(limit, with_energy):
        def run(p):
            late = push(p - UNROLL)
            fresh = pull(p, limit, with_energy)
            store(fresh)
            store(late)

        return run

    counted = -(-CA // UNROLL)

    def step(s, limit):
        first_plane = REACH * s
        store(pull(first_plane, limit, False))
        quiet = both_halves(limit, False)
        several(quiet, first_plane + UNROLL, sz.sections - 1 - s)
        several(both_halves(limit, True), halo, counted)
        several(quiet, halo + counted * UNROLL, sz.sections - 1 - s)
        store(push(halo + (counted + sz.sections - 2 - s) * UNROLL))
        return limit * (2.0**-12)

    for ref in (wait_a, wait_b):
        ref[...] = jnp.zeros_like(ref)
    lax.fori_loop(0, sz.sections, step, jnp.float32(1.0))

    half = lane < CZ // 2
    for c in range(3):
        for a in range(CA):
            at = pl.ds(c * CA * NR + a, NR, stride=CA)
            p = halo + a
            out_d[at, :] = jnp.where(half, fld[c, p, pl.ds(0, NR), :], fld[c, p, pl.ds(NR, NR), :])
            out_v[at, :] = jnp.where(half, fld[3 + c, p, pl.ds(0, NR), :], fld[3 + c, p, pl.ds(NR, NR), :])
    for b in range(CA // 2):
        up = energy[2 * b, pl.ds(0, NR), :] + energy[2 * b + 1, pl.ds(0, NR), :]
        dn = energy[2 * b, pl.ds(NR, NR), :] + energy[2 * b + 1, pl.ds(NR, NR), :]
        pooled[pl.ds(b * NR, NR), :] = jnp.where(half, up, dn) * (0.25 / sz.sections)
    mean = exact_dot(layers_of(), pooled[...], ((0,), (0,)))
    table = owner[...] * held + row_of[...]
    out_e[...] = exact_dot(wanted_rows(table, out_e.shape[0]), mean)


def call(body, ins, outs, scratch=(), name=None):
    arrays, spaces, parts = [], [], []
    for i in ins:
        x, how = i if isinstance(i, tuple) else (i, i.shape[0])
        staged = isinstance(how, int)
        arrays.append(pltpu.with_memory_space_constraint(x, pltpu.HBM) if staged else x)
        spaces.append(pltpu.HBM if staged else how)
        parts.append(how if staged else None)
    staged = [i for i, m in enumerate(parts) if m is not None]
    buffers = [pltpu.VMEM((parts[i],) + arrays[i].shape[1:], arrays[i].dtype) for i in staged]

    def kernel(*refs):
        refs = list(refs)
        sems = refs.pop()
        held = refs[len(refs) - len(staged) :]
        refs = refs[: len(refs) - len(staged)]
        copies = [
            pltpu.make_async_copy(refs[i].at[pl.ds(0, parts[i])], held[j], sems.at[j])
            for j, i in enumerate(staged)
        ]
        for c in copies:
            c.start()
        for j, i in enumerate(staged):
            refs[i] = held[j]
        for c in copies:
            c.wait()
        body(*refs)

    every = list(scratch) + buffers
    size = sum(math.prod(b.shape) * jnp.dtype(b.dtype).itemsize for b in every)
    size += sum(4 * math.prod(s) for s in outs)
    size += sum(4 * math.prod(a.shape) for a, m in zip(arrays, spaces) if m is pltpu.VMEM)
    return pl.pallas_call(
        kernel,
        name=name,
        out_shape=[jax.ShapeDtypeStruct(s, F32) for s in outs],
        in_specs=[pl.BlockSpec(memory_space=m) for m in spaces],
        out_specs=[pl.BlockSpec(memory_space=pltpu.VMEM)] * len(outs),
        scratch_shapes=every + [pltpu.SemaphoreType.DMA((max(1, len(staged)),))],
        compiler_params=pltpu.CompilerParams(vmem_limit_bytes=min(60 << 20, size + (6 << 20))),
    )(*arrays)


def on_device(displace, velocity, stiff, thermal, owner_of, row_of, breaks):
    sz = Sizes(breaks.shape[0])
    groups = lax.axis_size("axial")
    around = lax.axis_size("azim")
    held = thermal.shape[0]
    nreq = row_of.shape[-1]
    codes = breaks.reshape(sz.code_rows, CZ)
    owner = owner_of.reshape(1, nreq)
    local = row_of.reshape(1, nreq)
    disp = displace.transpose(0, 2, 1, 3).reshape(3 * NR * CA, CZ)
    velo = velocity.transpose(0, 2, 1, 3).reshape(3 * NR * CA, CZ)
    stif = stiff.transpose(1, 0, 2).reshape(NR * CA, CZ)

    edge, side, far = (sz.edge_rows, CZ), (sz.side_rows, CZ), (sz.far_rows, CZ)
    up, down, left, right, code_f = call(
        lambda *refs: pack_first(sz, held + 2 * sz.code_rows, *refs),
        [disp, velo, stif, codes, owner, local],
        [edge, edge, side, side, (sz.code_rows, CZ)],
        name="pack_first",
    )
    to_left = [(i, (i - 1) % around) for i in range(around)]
    to_right = [(i, (i + 1) % around) for i in range(around)]
    upward = [(i, i + 1) for i in range(groups - 1)]
    downward = [(i + 1, i) for i in range(groups - 1)]
    low = lax.ppermute(up, "axial", upward)
    high = lax.ppermute(down, "axial", downward)
    side_r = lax.ppermute(left, "azim", to_left)
    side_l = lax.ppermute(right, "azim", to_right)
    n = sz.code_rows
    share = held + 2 * n
    (out_box,) = call(
        lambda *refs: relay(groups, *refs),
        [thermal, (side_l, n), (side_r, n)],
        [(groups * share, CZ)],
        name="relay",
    )
    box = lax.all_to_all(out_box.reshape(groups, share, CZ), "axial", split_axis=0, concat_axis=0, tiled=True)

    plane = (PAIR, CZ)
    lanes = sz.code_rows * CZ
    tall = NBOND * CA // 4 * NR
    work = [
        pltpu.VMEM((tall, lanes), jnp.bfloat16),
        pltpu.VMEM((4 * CZ, lanes), jnp.bfloat16),
        pltpu.VMEM((tall + 2 * PAD, 4 * CZ), F32),
    ]
    (w_own,) = call(
        lambda *refs: breaks_own(sz, *refs), [code_f], [(NBOND, CA) + plane], work, name="breaks_own"
    )
    low, high, side_l, side_r, box, w_own = lax.optimization_barrier(
        (low, high, side_l, side_r, box, w_own)
    )
    left, right, temp = call(
        lambda *refs: pack_second(sz, held, share, *refs),
        [low, high, box.reshape(groups * share, CZ), owner, local],
        [far, far, (sz.temp_rows, CZ)],
        name="pack_second",
    )
    far_r = lax.ppermute(left, "azim", to_left)
    far_l = lax.ppermute(right, "azim", to_right)
    strip = -(-NBOND * PAIR // 16) * 16
    place = lax.axis_index("axial").astype(jnp.int32).reshape(1)

    def all_breaks(place, *refs):
        x = place[0]
        rows = [
            pl.multiple_of(jnp.clip(x + d, 0, groups - 1) * share + held, 8) for d in (-1, 1)
        ]
        breaks_all(sz, *rows, *refs)

    (broken,) = call(
        all_breaks,
        [(place, pltpu.SMEM), (w_own, pltpu.VMEM), (low, n), (high, n), (side_l, n), (side_r, n), box.reshape(groups * share, CZ)],
        [(NBOND, sz.ext) + plane],
        work
        + [
            pltpu.VMEM((strip, 2 * lanes), jnp.bfloat16),
            pltpu.VMEM((CA * SLOT, 2 * lanes), jnp.bfloat16),
            pltpu.VMEM((strip, CA * SLOT), F32),
        ],
        name="breaks_all",
    )
    planes = sz.ext + 2
    scratch = [
        pltpu.VMEM((NFIELD + 1, planes) + plane, F32),
        pltpu.VMEM((NBOND, sz.ext) + plane, F32),
        pltpu.VMEM((NBOND, sz.ext) + plane, F32),
        pltpu.VMEM((NBOND, UNROLL) + plane, F32),
        pltpu.VMEM((3, UNROLL) + plane, F32),
        pltpu.VMEM((REACH,) + plane, F32),
        pltpu.VMEM((2, REACH - 1) + plane, F32),
        pltpu.VMEM((-(-CA // UNROLL) * UNROLL,) + plane, F32),
        pltpu.VMEM((CA // 2 * NR, CZ), F32),
    ]
    total = groups * CA
    out_d, out_v, out_e = call(
        lambda *refs: march(sz, total, held, *refs),
        [
            (place, pltpu.SMEM), disp, velo, stif, low, high, temp, side_l, side_r, far_l, far_r, owner, local,
            (broken, pltpu.VMEM),
        ],
        [disp.shape, velo.shape, (groups * held, CZ)],
        scratch,
        name="march",
    )
    parts = out_e.reshape(groups, held, CZ)
    arrived = lax.all_to_all(parts, "axial", split_axis=0, concat_axis=0, tiled=True)
    shape = (3, NR, CA, CZ)
    return (
        out_d.reshape(shape).transpose(0, 2, 1, 3),
        out_v.reshape(shape).transpose(0, 2, 1, 3),
        jnp.sum(arrived, axis=0),
    )


def solution(mesh):
    return jax.shard_map(
        on_device,
        mesh=mesh,
        in_specs=(
            P(None, "axial", None, "azim"),
            P(None, "axial", None, "azim"),
            P("axial", None, "azim"),
            P("axial", "azim"),
            P("axial", "azim", None, None),
            P("axial", "azim", None),
            P(None, "axial", "azim", None),
        ),
        out_specs=(
            P(None, "axial", None, "azim"),
            P(None, "axial", None, "azim"),
            P("axial", "azim"),
        ),
        check_vma=False,
    )
```

```python
import math

import jax
import jax.numpy as jnp
from jax import lax
from jax.experimental import pallas as pl
from jax.experimental.pallas import tpu as pltpu
from jax.sharding import PartitionSpec as P

DILATION = 0.25
DT = 0.2
CA, NR, CZ = 16, 12, 128
REACH = 3
SLOT = 16
PAIR = 2 * NR
PAD = 16
PER = CZ // SLOT
UNROLL = 3
PREPARE = 13
NFIELD = 7
NEXACT = lax.Precision.HIGHEST
F32 = jnp.float32


def offset_table():
    table = []
    for da in range(REACH + 1):
        for dz in range(-REACH, REACH + 1):
            if da * da + dz * dz <= REACH * REACH and (da > 0 or dz > 0):
                table.append((da, 0, dz))
    table.append((0, 1, 0))
    return table


OFFSETS = offset_table()
NBOND = len(OFFSETS)
NUMBER = {o: i for i, o in enumerate(OFFSETS)}


def scales(o):
    return sum(x * x for x in o), math.gcd(math.gcd(o[0], o[1]), abs(o[2]))


def roll(x, shift, axis=1):
    shift %= x.shape[axis]
    return pltpu.roll(x, shift, axis) if shift else x


def lanes_of(shape=(NR, CZ)):
    return lax.broadcasted_iota(jnp.int32, shape, 1)


def dot_nt(a, b):
    return lax.dot_general(a, b, (((1,), (1,)), ((), ())), preferred_element_type=F32)


class Sizes:
    def __init__(self, sections, rows):
        self.sections = sections
        self.halo = REACH * sections
        self.ext = CA + 2 * self.halo
        self.code_rows = 4 * sections
        self.edge_at = {}
        at = PAD
        for f in range(NFIELD):
            for e in range(self.halo):
                if not self.moving(f) or e < self.halo - REACH:
                    self.edge_at[f, e] = at
                    at += NR
        self.tab_at = -(-at // 8) * 8
        self.edge_rows = self.tab_at + PAD
        self.own_tiles = CA // PER
        self.side_heat = -(-(PAD + NFIELD * self.own_tiles * NR + NR) // 8) * 8
        self.side_tab = self.side_heat + rows
        self.side_rows = self.side_tab + 8
        self.table = CA // 2 * NR

    def moving(self, f):
        return 3 <= f < 6

    def edge_row(self, f, p):
        e = p if p < self.halo else p - self.halo - CA
        if self.moving(f) and p < self.halo:
            e -= REACH
        return self.edge_at.get((f, e))

    def source(self, p):
        if p < self.halo:
            return 0, CA - self.halo + p
        if p < self.halo + CA:
            return 1, p - self.halo
        return 2, p - self.halo - CA

    def side_row(self, f, t):
        return PAD + (f * self.own_tiles + t) * NR


def own_plane(refs, f, a):
    disp, velo, stiff = refs
    ref, g = (disp, f) if f < 3 else (velo, f - 3) if f < 6 else (stiff, 0)
    return ref[pl.ds(g * CA * NR + a, NR, stride=CA), :]


def is_top():
    return lax.broadcasted_iota(jnp.int32, (PAIR, CZ), 0) < NR


def twice(upper, lower, at, low_at=None):
    low_at = at if low_at is None else low_at
    return jnp.where(is_top(), upper[pl.ds(at, PAIR), :], lower[pl.ds(low_at - NR, PAIR), :])


def wanted_rows(table, count):
    rows = lax.broadcasted_iota(jnp.int32, (count, table.shape[1]), 0)
    return (rows == table).astype(F32)


def layers_of():
    shape = (CA // 2 * NR, CA // 2 * NR // 2)
    i = lax.broadcasted_iota(jnp.int32, shape, 0)
    j = lax.broadcasted_iota(jnp.int32, shape, 1)
    return (i // 2 == j).astype(F32)


def exact_dot(a, b, dims=((1,), (0,))):
    return lax.dot_general(a, b, (dims, ((), ())), precision=NEXACT, preferred_element_type=F32)


def pack_tiles(sz, planes, left, right, row):
    lane = lanes_of()
    to_left = to_right = None
    for s, x in enumerate(planes):
        if x is None:
            continue
        x = roll(x, SLOT * (s + 1))
        if to_left is None:
            to_left = to_right = x
            continue
        to_right = jnp.where(lane >= SLOT * s, x, to_right)
        n = (s + 1) % PER
        to_left = jnp.where((lane >= SLOT * n) & (lane < SLOT * (n + 1)), x, to_left)
    left[pl.ds(row, NR), :] = to_left
    right[pl.ds(row, NR), :] = to_right


def pack_first(sz, share, disp, velo, stiff, codes, owner, row_of, thermal, up, down, left, right, code_f):
    refs = (disp, velo, stiff)
    for f in range(NFIELD):
        for p in range(sz.halo):
            at = sz.edge_row(f, p)
            if at is not None:
                up[pl.ds(at, NR), :] = own_plane(refs, f, CA - sz.halo + p)
            at = sz.edge_row(f, p + sz.halo + CA)
            if at is not None:
                down[pl.ds(at, NR), :] = own_plane(refs, f, p)
        for t in range(sz.own_tiles):
            planes = [own_plane(refs, f, t * PER + s) for s in range(PER)]
            pack_tiles(sz, planes, left, right, sz.side_row(f, t))
    c = codes[...].astype(F32)
    code_f[...] = c
    wanted = (owner[...] * share + row_of[...]).astype(F32)
    wanted = jnp.broadcast_to(wanted, (8, wanted.shape[1]))
    table = exact_dot(wanted, layers_of(), ((1,), (1,)))
    for out in (up, down, left, right):
        out[pl.ds(0, sz.code_rows), :] = c
    for out, at in ((up, sz.tab_at), (down, sz.tab_at), (left, sz.side_tab), (right, sz.side_tab)):
        out[pl.ds(at, 8), pl.ds(0, sz.table)] = table
    for out in (left, right):
        out[pl.ds(sz.side_heat, thermal.shape[0]), :] = thermal[...]


def relay(sz, groups, thermal, side_l, side_r, box, ring):
    rows = thermal.shape[0]
    n = sz.code_rows
    heat = pl.ds(sz.side_heat, rows)
    beside = jnp.where(lanes_of((rows, CZ)) < CZ // 2, side_r[heat, :], side_l[heat, :])
    for g in range(groups):
        at = g * (2 * rows + 2 * n)
        box[pl.ds(at, rows), :] = thermal[...]
        box[pl.ds(at + rows, rows), :] = beside
        box[pl.ds(at + 2 * rows, n), :] = side_l[pl.ds(0, n), :]
        box[pl.ds(at + 2 * rows + n, n), :] = side_r[pl.ds(0, n), :]
    ring[pl.ds(0, sz.side_rows), :] = side_l[...]
    ring[pl.ds(sz.side_rows, sz.side_rows), :] = side_r[...]


def decode(codes):
    hi = jnp.floor(codes * (1.0 / CZ))
    z = codes - hi * CZ
    k = jnp.floor((hi + 0.5) * (1.0 / (CA * NR)))
    rest = hi - k * (CA * NR)
    a = jnp.floor((rest + 0.5) * (1.0 / NR))
    return k, a, rest - a * NR, z


def spread(ref, index, rows, chunk, lane_at=0, weigh=False):
    for first in range(0, rows, chunk):
        size = min(chunk, rows - first)
        near = jnp.clip(index - first, -1.0, 256.0)
        at = lax.broadcasted_iota(jnp.int32, (size, CZ), 0).astype(F32).astype(jnp.bfloat16)
        for i in range(index.shape[0]):
            w = jnp.full((size, CZ), 2.0 ** (-12 * (i // 4)) if weigh else 1.0, jnp.bfloat16)
            here = jnp.broadcast_to(near[i : i + 1, :], (size, CZ)).astype(jnp.bfloat16)
            ref[pl.ds(first, size), pl.ds(lane_at + i * CZ, CZ)] = jnp.where(
                at == here, w, jnp.zeros_like(w)
            )


def read_breaks(sz, parts, out, rows_ref, cols_ref, acc):
    for src, lo_group, groups, first, count, at in parts:
        k, a, r, z = decode(src)
        group = jnp.floor(a * 0.25)
        per_k = groups * NR
        rows = -(-NBOND * per_k // 16) * 16
        inside = (group >= lo_group) & (group < lo_group + groups)
        index = jnp.where(inside, k * per_k + (group - lo_group) * NR + r, -1.0)
        spread(rows_ref, index, rows, 240)
        spread(cols_ref, (a - 4 * group) * CZ + z, 4 * CZ, CZ * 2, weigh=True)
        acc[pl.ds(PAD, rows), :] = dot_nt(rows_ref[pl.ds(0, rows), :], cols_ref[...])
        for b in range(NBOND):
            for i in range(count):
                plane = first + i
                row = PAD + b * per_k + (plane // 4 - lo_group) * NR
                lanes = pl.ds(plane % 4 * CZ, CZ)
                out[b, at + i] = jnp.where(
                    is_top(), acc[pl.ds(row, PAIR), lanes], acc[pl.ds(row - NR, PAIR), lanes]
                )


def breaks_own(sz, codes, out, rows_ref, cols_ref, acc):
    acc[pl.ds(0, PAD), :] = jnp.zeros((PAD, 4 * CZ), F32)
    read_breaks(sz, [(codes[...], 0, CA // 4, 0, CA, 0)], out, rows_ref, cols_ref, acc)


def breaks_all(
    sz, at_lo, at_hi, own, low, high, side_l, side_r, box, out, rows_ref, cols_ref, acc, rows_s, cols_s, acc_l, acc_r
):
    n, halo = sz.code_rows, sz.halo
    acc[pl.ds(0, PAD), :] = jnp.zeros((PAD, 4 * CZ), F32)
    parts = [
        (low[...], (CA - halo) // 4, halo // 4, CA - halo, halo, 0),
        (high[...], 0, halo // 4, 0, halo, halo + CA),
    ]
    read_breaks(sz, parts, out, rows_ref, cols_ref, acc)
    wide = lanes_of((PAIR, CZ))
    edge = (is_top() & (wide >= CZ - SLOT)) | (~is_top() & (wide < SLOT))
    sources = [
        (box[pl.ds(at_lo, n), :], box[pl.ds(at_lo + n, n), :]),
        (side_l[pl.ds(0, n), :], side_r[pl.ds(0, n), :]),
        (box[pl.ds(at_hi, n), :], box[pl.ds(at_hi + n, n), :]),
    ]
    side_breaks(sz, sources, own, out, rows_s, cols_s, acc_l, acc_r, edge)


def side_breaks(sz, sources, own, out, rows_ref, cols_ref, acc_l, acc_r, edge):
    rows = -(-NBOND * NR // 16) * 16
    for which, (left, right) in enumerate(sources):
        first = CA - sz.halo if which == 0 else 0
        count = CA if which == 1 else sz.halo
        cols = -(-count // PER) * CZ
        for side, codes in enumerate((left, right)):
            k, a, r, z = decode(codes)
            spread(rows_ref, k * NR + r, rows, 192)
            a = a - first
            tile = jnp.floor(a * (1.0 / PER))
            slot = a - tile * PER + side
            slot = jnp.where(slot == PER, 0.0, slot)
            lane = z if side else z - (CZ - SLOT)
            near = (lane >= 0) & (lane < SLOT) & (a >= 0) & (a < count)
            spread(cols_ref, jnp.where(near, tile * CZ + slot * SLOT + lane, -1.0), cols, 256, weigh=True)
            acc = acc_r if side else acc_l
            acc[pl.ds(PAD, rows), pl.ds(0, cols)] = dot_nt(rows_ref[...], cols_ref[pl.ds(0, cols), :])
        for b in range(NBOND):
            for t in range(cols // CZ):
                lanes = pl.ds(t * CZ, CZ)
                x = jnp.where(
                    is_top(), acc_l[pl.ds(PAD + b * NR, PAIR), lanes], acc_r[pl.ds(PAD + b * NR - NR, PAIR), lanes]
                )
                for s in range(min(PER, count - t * PER)):
                    i = t * PER + s
                    p = i + (0, sz.halo, sz.halo + CA)[which]
                    old = own[b, i] if which == 1 else out[b, p]
                    out[b, p] = jnp.where(edge, roll(x, SLOT * (PER - 1 - s)), old)


def march(
    sz, total, held, place, disp, velo, stiff, low, high, side_l, side_r, ring_lo, ring_hi, owner, row_of,
    box, broken, out_d, out_v, out_e, fld, stiffk, heatk, bonds, forces, wait_a, wait_b, energy, pooled, temp, tables,
):
    refs = (disp, velo, stiff)
    halo = sz.halo
    lane = lanes_of()
    wide = lanes_of((PAIR, CZ))
    top = is_top()
    edge = (top & (wide >= CZ - SLOT)) | (~top & (wide < SLOT))
    share = 2 * (held + sz.code_rows)
    heat = box[...]
    wanted = (owner[...] * share + row_of[...]).astype(F32)
    wanted = exact_dot(jnp.broadcast_to(wanted, (8, wanted.shape[1])), layers_of(), ((1,), (1,)))
    lists = {
        (0, 1): low[pl.ds(sz.tab_at, 8), pl.ds(0, sz.table)],
        (1, 1): wanted,
        (2, 1): high[pl.ds(sz.tab_at, 8), pl.ds(0, sz.table)],
    }
    for which, ref, at in (
        (0, ring_lo, 0), (0, ring_lo, sz.side_rows), (1, side_l, 0), (1, side_r, 0), (2, ring_hi, 0), (2, ring_hi, sz.side_rows)
    ):
        side = 2 if at or ref is side_r else 0
        lists[which, side] = ref[pl.ds(at + sz.side_tab, 8), pl.ds(0, sz.table)] + held
    parts, rest = [], heat
    for _ in range(3):
        part = rest.astype(jnp.bfloat16)
        parts.append(part)
        rest = rest - part.astype(F32)
    heat3 = jnp.concatenate(parts, axis=1)
    for j, (key, table) in enumerate(lists.items()):
        tables[pl.ds(j, 1), pl.ds(0, sz.table)] = table[0:1]
    columns = tables[...].T
    row_id = lax.broadcasted_iota(jnp.int32, (sz.table, heat.shape[0]), 1).astype(F32)
    for j, (which, side) in enumerate(lists):
        hot = jnp.where(columns[0 : sz.table, j : j + 1] == row_id, 1.0, 0.0).astype(jnp.bfloat16)
        got = jnp.dot(hot, heat3, preferred_element_type=F32)
        temp[3 * which + side, pl.ds(PAD, sz.table), :] = (
            got[:, 0:CZ] + got[:, CZ : 2 * CZ] + got[:, 2 * CZ :]
        )
    for p in range(sz.ext):
        which, a = sz.source(p)
        for f in range(NFIELD):
            if which == 1:
                x = own_plane(refs, f, a)
                x = jnp.concatenate([x, x], axis=0)
                y = twice(side_l, side_r, sz.side_row(f, a // PER))
            else:
                at = sz.edge_row(f, p)
                if at is None:
                    continue
                src = low if which == 0 else high
                x = twice(src, src, at)
                ring = ring_lo if which == 0 else ring_hi
                at = sz.side_row(f, a // PER)
                y = twice(ring, ring, at, at + sz.side_rows)
            fld[f, p] = jnp.where(edge, roll(y, SLOT * (PER - 1 - a % PER)), x)
        at = PAD + a // 2 * NR
        x = twice(temp.at[3 * which + 1], temp.at[3 * which + 1], at)
        y = twice(temp.at[3 * which], temp.at[3 * which + 2], at)
        fld[NFIELD, p] = jnp.where(edge, y, x)

    row = lax.broadcasted_iota(jnp.int32, (PAIR, CZ), 0)
    not_top = jnp.where((row == NR - 1) | (row == PAIR - 1), 0.0, 1.0)
    start = place[0] * CA - halo

    def turned(cache, f, p, i, dz):
        key = f, i, dz
        if key not in cache:
            x = turned(cache, f, p, i, 0) if dz else fld[f, p + i]
            cache[key] = roll(x, -dz)
        return cache[key]

    def prepare(p):
        cache = {}
        get = lambda f, i, dz=0: turned(cache, f, p, i, dz)
        for i in range(PREPARE):
            at = start + p + i
            live = [
                jnp.where((at >= 0) & (at + da < total), 1.0, 0.0).astype(F32) for da in range(REACH + 1)
            ]
            c, h = get(6, i), get(7, i)
            for k, (da, dr, dz) in enumerate(OFFSETS):
                n2, d = scales((da, dr, dz))
                if dr:
                    c2, h2 = roll(c, -1, 0), roll(h, -1, 0)
                else:
                    c2, h2 = get(6, i + da, dz), get(7, i + da, dz)
                m = (c + c2) * (live[da] * (0.5 * d * d / (n2 * n2)))
                stiffk[k, p + i] = m * not_top if dr else m
                heatk[k, p + i] = (h + h2) * (DILATION * 0.5 * n2 / d)

    def several(body, first_plane, times, group=UNROLL):
        def one(i, c):
            body(first_plane + i * group)
            return c

        lax.fori_loop(0, times, one, 0)

    several(prepare, 0, (sz.ext - 1) // PREPARE, PREPARE)
    energy[...] = jnp.zeros_like(energy)

    span = range(UNROLL)

    def pull(p, limit, with_energy):
        cache = {}
        get = lambda f, i, dz=0: turned(cache, f, p, i, dz)
        fa_at = {i: wait_a[i] for i in range(REACH)}
        fz_at = {}
        sums = [{} for _ in span]
        keep = []

        def add(to, i, x):
            to[i] = to[i] + x if i in to else x

        def bond(i, o, elongation):
            k = NUMBER[o]
            q = elongation - heatk[k, p + i]
            g = jnp.where(broken[k, p + i] >= limit, 0.0, stiffk[k, p + i]) * q
            if with_energy:
                add(sums[i], scales(o)[0], g * q)
            if o[2]:
                keep.append((bonds, (k, i), g))
            return g

        for i in span:
            ua, ur, uz = get(0, i), get(1, i), get(2, i)
            for dz in (1, 2, 3):
                add(fz_at, i, bond(i, (0, 0, dz), get(2, i, dz) - uz))
            g = bond(i, (0, 1, 0), roll(ur, -1, 0) - ur)
            keep.append((forces, (1, i), g - roll(g, 1, 0)))
            for da in (1, 2):
                j = i + da
                g = bond(i, (da, 0, 0), get(0, j) - ua)
                add(fa_at, i, g)
                add(fa_at, j, -g)
                for dz in (1, 2):
                    gs = []
                    for sign in (1, -1):
                        dua = get(0, j, sign * dz) - ua
                        duz = get(2, j, sign * dz) - uz
                        if da == dz:
                            e = dua + duz if sign > 0 else dua - duz
                        elif dz == 2:
                            e = dua + (2.0 * sign) * duz
                        else:
                            e = 2.0 * dua + duz if sign > 0 else 2.0 * dua - duz
                        gs.append(bond(i, (da, 0, sign * dz), e))
                    own_s, own_d = gs[0] + gs[1], gs[0] - gs[1]
                    add(fa_at, i, own_s if da in (1, dz) else float(da) * own_s)
                    add(fz_at, i, own_d if dz in (1, da) else float(dz) * own_d)
            g = bond(i, (3, 0, 0), get(0, i + 3) - ua)
            add(fa_at, i, g)
            add(fa_at, i + 3, -g)
            keep.append((forces, (0, i), fa_at[i]))
            keep.append((forces, (2, i), fz_at[i]))
        keep += [(wait_a, (i,), fa_at[i + UNROLL]) for i in range(REACH)]
        if with_energy:
            for i in span:
                e = None
                for n2, x in sums[i].items():
                    y = x * (0.5 / math.sqrt(n2))
                    e = y if e is None else e + y
                keep.append((energy, (p + i - halo,), energy[p + i - halo] + e))
        return keep

    def push(p):
        fa_at = {i: wait_b[0, i] for i in range(REACH - 1)}
        fz_at = {i: wait_b[1, i] for i in range(REACH - 1)}
        keep = []

        def add(to, i, x):
            to[i] = to[i] + x if i in to else x

        for i in span:
            for da in (0, 1, 2):
                j = i + da
                for dz in (1, 2) if da else (1, 2, 3):
                    plus = roll(bonds[NUMBER[da, 0, dz], i], dz)
                    if da == 0:
                        add(fz_at, j, plus)
                        continue
                    minus = roll(bonds[NUMBER[da, 0, -dz], i], -dz)
                    both, gap = plus + minus, plus - minus
                    add(fa_at, j, both if da in (1, dz) else float(da) * both)
                    add(fz_at, j, gap if dz in (1, da) else float(dz) * gap)
            for f, force in (
                (0, forces[0, i] - fa_at[i]),
                (1, forces[1, i]),
                (2, forces[2, i] - fz_at[i]),
            ):
                v = fld[3 + f, p + i] + DT * force
                keep.append((fld, (3 + f, p + i), v))
                keep.append((fld, (f, p + i), fld[f, p + i] + DT * v))
        for i in range(REACH - 1):
            keep.append((wait_b, (0, i), fa_at[UNROLL + i]))
            keep.append((wait_b, (1, i), fz_at[UNROLL + i]))
        return keep

    def store(keep):
        for ref, index, value in keep:
            ref[index] = value

    def both_halves(limit, with_energy):
        def run(p):
            late = push(p - UNROLL)
            fresh = pull(p, limit, with_energy)
            store(fresh)
            store(late)

        return run

    counted = -(-CA // UNROLL)

    def step(s, limit):
        first_plane = REACH * s
        store(pull(first_plane, limit, False))
        quiet = both_halves(limit, False)
        several(quiet, first_plane + UNROLL, sz.sections - 1 - s)
        several(both_halves(limit, True), halo, counted)
        several(quiet, halo + counted * UNROLL, sz.sections - 1 - s)
        store(push(halo + (counted + sz.sections - 2 - s) * UNROLL))
        return limit * (2.0**-12)

    for ref in (wait_a, wait_b):
        ref[...] = jnp.zeros_like(ref)
    lax.fori_loop(0, sz.sections, step, jnp.float32(1.0))

    half = lane < CZ // 2
    for c in range(3):
        for a in range(CA):
            at = pl.ds(c * CA * NR + a, NR, stride=CA)
            p = halo + a
            out_d[at, :] = jnp.where(half, fld[c, p, pl.ds(0, NR), :], fld[c, p, pl.ds(NR, NR), :])
            out_v[at, :] = jnp.where(half, fld[3 + c, p, pl.ds(0, NR), :], fld[3 + c, p, pl.ds(NR, NR), :])
    for b in range(CA // 2):
        up = energy[2 * b, pl.ds(0, NR), :] + energy[2 * b + 1, pl.ds(0, NR), :]
        dn = energy[2 * b, pl.ds(NR, NR), :] + energy[2 * b + 1, pl.ds(NR, NR), :]
        pooled[pl.ds(b * NR, NR), :] = jnp.where(half, up, dn) * (0.25 / sz.sections)
    mean = exact_dot(layers_of(), pooled[...], ((0,), (0,)))
    table = owner[...] * held + row_of[...]
    out_e[...] = exact_dot(wanted_rows(table, out_e.shape[0]), mean)


def call(body, ins, outs, scratch=(), name=None):
    arrays, spaces, parts = [], [], []
    for i in ins:
        x, how = i if isinstance(i, tuple) else (i, i.shape[0])
        staged = isinstance(how, int)
        arrays.append(pltpu.with_memory_space_constraint(x, pltpu.HBM) if staged else x)
        spaces.append(pltpu.HBM if staged else how)
        parts.append(how if staged else None)
    staged = [i for i, m in enumerate(parts) if m is not None]
    buffers = [pltpu.VMEM((parts[i],) + arrays[i].shape[1:], arrays[i].dtype) for i in staged]

    def kernel(*refs):
        refs = list(refs)
        sems = refs.pop()
        held = refs[len(refs) - len(staged) :]
        refs = refs[: len(refs) - len(staged)]
        copies = [
            pltpu.make_async_copy(refs[i].at[pl.ds(0, parts[i])], held[j], sems.at[j])
            for j, i in enumerate(staged)
        ]
        for c in copies:
            c.start()
        for j, i in enumerate(staged):
            refs[i] = held[j]
        for c in copies:
            c.wait()
        body(*refs)

    every = list(scratch) + buffers
    size = sum(math.prod(b.shape) * 4 for b in every)
    size += sum(4 * math.prod(s) for s in outs)
    size += sum(4 * math.prod(a.shape) for a, m in zip(arrays, spaces) if m is pltpu.VMEM)
    return pl.pallas_call(
        kernel,
        name=name,
        out_shape=[jax.ShapeDtypeStruct(s, F32) for s in outs],
        in_specs=[pl.BlockSpec(memory_space=m) for m in spaces],
        out_specs=[pl.BlockSpec(memory_space=pltpu.VMEM)] * len(outs),
        scratch_shapes=every + [pltpu.SemaphoreType.DMA((max(1, len(staged)),))],
        compiler_params=pltpu.CompilerParams(vmem_limit_bytes=min(60 << 20, size + (6 << 20))),
    )(*arrays)


def on_device(displace, velocity, stiff, thermal, owner_of, row_of, breaks):
    sz = Sizes(breaks.shape[0], thermal.shape[0])
    groups = lax.axis_size("axial")
    around = lax.axis_size("azim")
    held = thermal.shape[0]
    nreq = row_of.shape[-1]
    codes = breaks.reshape(sz.code_rows, CZ)
    owner = owner_of.reshape(1, nreq)
    local = row_of.reshape(1, nreq)
    disp = displace.transpose(0, 2, 1, 3).reshape(3 * NR * CA, CZ)
    velo = velocity.transpose(0, 2, 1, 3).reshape(3 * NR * CA, CZ)
    stif = stiff.transpose(1, 0, 2).reshape(NR * CA, CZ)

    edge, side = (sz.edge_rows, CZ), (sz.side_rows, CZ)
    n = sz.code_rows
    share = 2 * (held + n)
    up, down, left, right, code_f = call(
        lambda *refs: pack_first(sz, share, *refs),
        [disp, velo, stif, codes, owner, local, thermal],
        [edge, edge, side, side, (n, CZ)],
        name="pack_first",
    )
    to_left = [(i, (i - 1) % around) for i in range(around)]
    to_right = [(i, (i + 1) % around) for i in range(around)]
    upward = [(i, i + 1) for i in range(groups - 1)]
    downward = [(i + 1, i) for i in range(groups - 1)]
    low = lax.ppermute(up, "axial", upward)
    high = lax.ppermute(down, "axial", downward)
    side_r = lax.ppermute(left, "azim", to_left)
    side_l = lax.ppermute(right, "azim", to_right)
    plane = (PAIR, CZ)
    lanes = n * CZ
    tall = NBOND * CA // 4 * NR
    work = [
        pltpu.VMEM((tall, lanes), jnp.bfloat16),
        pltpu.VMEM((4 * CZ, lanes), jnp.bfloat16),
        pltpu.VMEM((tall + 2 * PAD, 4 * CZ), F32),
    ]
    (w_own,) = call(
        lambda *refs: breaks_own(sz, *refs),
        [(code_f, pltpu.VMEM)],
        [(NBOND, CA) + plane],
        work,
        name="breaks_own",
    )
    side_l, side_r, w_own = lax.optimization_barrier((side_l, side_r, w_own))
    out_box, ring = call(
        lambda *refs: relay(sz, groups, *refs),
        [thermal, (side_l, pltpu.VMEM), (side_r, pltpu.VMEM)],
        [(groups * share, CZ), (2 * sz.side_rows, CZ)],
        name="relay",
    )
    ring_lo = lax.ppermute(ring, "axial", upward)
    ring_hi = lax.ppermute(ring, "axial", downward)
    box = lax.all_to_all(out_box.reshape(groups, share, CZ), "axial", split_axis=0, concat_axis=0, tiled=True)
    box = box.reshape(groups * share, CZ)
    strip = -(-NBOND * NR // 16) * 16
    place = lax.axis_index("axial").astype(jnp.int32).reshape(1)

    def all_breaks(place, *refs):
        x = place[0]
        rows = [
            pl.multiple_of(jnp.clip(x + d, 0, groups - 1) * share + 2 * held, 8) for d in (-1, 1)
        ]
        breaks_all(sz, *rows, *refs)

    (broken,) = call(
        all_breaks,
        [(place, pltpu.SMEM), (w_own, pltpu.VMEM), (low, n), (high, n), (side_l, pltpu.VMEM), (side_r, pltpu.VMEM), (box, pltpu.VMEM)],
        [(NBOND, sz.ext) + plane],
        work
        + [
            pltpu.VMEM((strip, lanes), jnp.bfloat16),
            pltpu.VMEM((CA * SLOT, lanes), jnp.bfloat16),
            pltpu.VMEM((strip + 2 * PAD, CA * SLOT), F32),
            pltpu.VMEM((strip + 2 * PAD, CA * SLOT), F32),
        ],
        name="breaks_all",
    )
    planes = sz.ext + 2
    scratch = [
        pltpu.VMEM((NFIELD + 1, planes) + plane, F32),
        pltpu.VMEM((NBOND, sz.ext) + plane, F32),
        pltpu.VMEM((NBOND, sz.ext) + plane, F32),
        pltpu.VMEM((NBOND, UNROLL) + plane, F32),
        pltpu.VMEM((3, UNROLL) + plane, F32),
        pltpu.VMEM((REACH,) + plane, F32),
        pltpu.VMEM((2, REACH - 1) + plane, F32),
        pltpu.VMEM((-(-CA // UNROLL) * UNROLL,) + plane, F32),
        pltpu.VMEM((CA // 2 * NR, CZ), F32),
        pltpu.VMEM((9, PAD + sz.table + PAD, CZ), F32),
        pltpu.VMEM((CZ, CZ), F32),
    ]
    total = groups * CA
    out_d, out_v, out_e = call(
        lambda *refs: march(sz, total, held, *refs),
        [
            (place, pltpu.SMEM), disp, velo, stif, low, high, (side_l, pltpu.VMEM), (side_r, pltpu.VMEM), ring_lo, ring_hi, owner, local,
            (box, pltpu.VMEM), (broken, pltpu.VMEM),
        ],
        [disp.shape, velo.shape, (groups * held, CZ)],
        scratch,
        name="march",
    )
    parts = out_e.reshape(groups, held, CZ)
    arrived = lax.all_to_all(parts, "axial", split_axis=0, concat_axis=0, tiled=True)
    shape = (3, NR, CA, CZ)
    return (
        out_d.reshape(shape).transpose(0, 2, 1, 3),
        out_v.reshape(shape).transpose(0, 2, 1, 3),
        jnp.sum(arrived, axis=0),
    )


def solution(mesh):
    return jax.shard_map(
        on_device,
        mesh=mesh,
        in_specs=(
            P(None, "axial", None, "azim"),
            P(None, "axial", None, "azim"),
            P("axial", None, "azim"),
            P("axial", "azim"),
            P("axial", "azim", None, None),
            P("axial", "azim", None),
            P(None, "axial", "azim", None),
        ),
        out_specs=(
            P(None, "axial", None, "azim"),
            P(None, "axial", None, "azim"),
            P("axial", "azim"),
        ),
        check_vma=False,
    )
```

```python
import math

import jax
import jax.numpy as jnp
from jax import lax
from jax.experimental import pallas as pl
from jax.experimental.pallas import tpu as pltpu
from jax.sharding import PartitionSpec as P

DILATION = 0.25
DT = 0.2
CA, NR, CZ = 16, 12, 128
REACH = 3
SLOT = 16
PAIR = 2 * NR
PAD = 16
PER = CZ // SLOT
UNROLL = 3
PREPARE = 13
NFIELD = 7
NEXACT = lax.Precision.HIGHEST
F32 = jnp.float32


def offset_table():
    table = []
    for da in range(REACH + 1):
        for dz in range(-REACH, REACH + 1):
            if da * da + dz * dz <= REACH * REACH and (da > 0 or dz > 0):
                table.append((da, 0, dz))
    table.append((0, 1, 0))
    return table


OFFSETS = offset_table()
NBOND = len(OFFSETS)
NUMBER = {o: i for i, o in enumerate(OFFSETS)}


def scales(o):
    return sum(x * x for x in o), math.gcd(math.gcd(o[0], o[1]), abs(o[2]))


def roll(x, shift, axis=1):
    shift %= x.shape[axis]
    return pltpu.roll(x, shift, axis) if shift else x


def lanes_of(shape=(NR, CZ)):
    return lax.broadcasted_iota(jnp.int32, shape, 1)


def dot_nt(a, b):
    return lax.dot_general(a, b, (((1,), (1,)), ((), ())), preferred_element_type=F32)


class Sizes:
    def __init__(self, sections, rows):
        self.sections = sections
        self.halo = REACH * sections
        self.ext = CA + 2 * self.halo
        self.code_rows = 4 * sections
        self.edge_at = {}
        at = PAD
        for f in range(NFIELD):
            for e in range(self.halo):
                if not self.moving(f) or e < self.halo - REACH:
                    self.edge_at[f, e] = at
                    at += NR
        self.tab_at = -(-at // 8) * 8
        self.edge_rows = self.tab_at + PAD
        self.own_tiles = CA // PER
        self.side_heat = -(-(PAD + NFIELD * self.own_tiles * NR + NR) // 8) * 8
        self.side_tab = self.side_heat + rows
        self.side_rows = self.side_tab + 8
        self.table = CA // 2 * NR

    def moving(self, f):
        return 3 <= f < 6

    def edge_row(self, f, p):
        e = p if p < self.halo else p - self.halo - CA
        if self.moving(f) and p < self.halo:
            e -= REACH
        return self.edge_at.get((f, e))

    def source(self, p):
        if p < self.halo:
            return 0, CA - self.halo + p
        if p < self.halo + CA:
            return 1, p - self.halo
        return 2, p - self.halo - CA

    def side_row(self, f, t):
        return PAD + (f * self.own_tiles + t) * NR


def own_plane(refs, f, a):
    disp, velo, stiff = refs
    ref, g = (disp, f) if f < 3 else (velo, f - 3) if f < 6 else (stiff, 0)
    return ref[pl.ds(g * CA * NR + a, NR, stride=CA), :]


def is_top():
    return lax.broadcasted_iota(jnp.int32, (PAIR, CZ), 0) < NR


def twice(upper, lower, at, low_at=None):
    low_at = at if low_at is None else low_at
    return jnp.where(is_top(), upper[pl.ds(at, PAIR), :], lower[pl.ds(low_at - NR, PAIR), :])


def wanted_rows(table, count):
    rows = lax.broadcasted_iota(jnp.int32, (count, table.shape[1]), 0)
    return (rows == table).astype(F32)


def layers_of():
    shape = (CA // 2 * NR, CA // 2 * NR // 2)
    i = lax.broadcasted_iota(jnp.int32, shape, 0)
    j = lax.broadcasted_iota(jnp.int32, shape, 1)
    return (i // 2 == j).astype(F32)


def exact_dot(a, b, dims=((1,), (0,))):
    return lax.dot_general(a, b, (dims, ((), ())), precision=NEXACT, preferred_element_type=F32)


def pack_tiles(sz, planes, left, right, row):
    lane = lanes_of()
    to_left = to_right = None
    for s, x in enumerate(planes):
        if x is None:
            continue
        x = roll(x, SLOT * (s + 1))
        if to_left is None:
            to_left = to_right = x
            continue
        to_right = jnp.where(lane >= SLOT * s, x, to_right)
        n = (s + 1) % PER
        to_left = jnp.where((lane >= SLOT * n) & (lane < SLOT * (n + 1)), x, to_left)
    left[pl.ds(row, NR), :] = to_left
    right[pl.ds(row, NR), :] = to_right


def pack_first(sz, share, disp, velo, stiff, codes, owner, row_of, thermal, up, down, left, right, code_f):
    refs = (disp, velo, stiff)
    for f in range(NFIELD):
        for p in range(sz.halo):
            at = sz.edge_row(f, p)
            if at is not None:
                up[pl.ds(at, NR), :] = own_plane(refs, f, CA - sz.halo + p)
            at = sz.edge_row(f, p + sz.halo + CA)
            if at is not None:
                down[pl.ds(at, NR), :] = own_plane(refs, f, p)
        for t in range(sz.own_tiles):
            planes = [own_plane(refs, f, t * PER + s) for s in range(PER)]
            pack_tiles(sz, planes, left, right, sz.side_row(f, t))
    c = codes[...].astype(F32)
    code_f[...] = c
    wanted = (owner[...] * share + row_of[...]).astype(F32)
    wanted = jnp.broadcast_to(wanted, (8, wanted.shape[1]))
    table = exact_dot(wanted, layers_of(), ((1,), (1,)))
    for out in (up, down, left, right):
        out[pl.ds(0, sz.code_rows), :] = c
    for out, at in ((up, sz.tab_at), (down, sz.tab_at), (left, sz.side_tab), (right, sz.side_tab)):
        out[pl.ds(at, 8), pl.ds(0, sz.table)] = table
    for out in (left, right):
        out[pl.ds(sz.side_heat, thermal.shape[0]), :] = thermal[...]


def relay(sz, groups, thermal, side_l, side_r, ring, box, share, sems, ring_sems):
    rows = thermal.shape[0]
    n = sz.code_rows
    copies = [
        pltpu.make_async_copy(side, ring.at[pl.ds(i * sz.side_rows, sz.side_rows)], ring_sems.at[i])
        for i, side in enumerate((side_l, side_r))
    ]
    for c in copies:
        c.start()
    heat = pl.ds(sz.side_heat, rows)
    share[pl.ds(0, rows), :] = thermal[...]
    share[pl.ds(rows, rows), :] = jnp.where(
        lanes_of((rows, CZ)) < CZ // 2, side_r[heat, :], side_l[heat, :]
    )
    share[pl.ds(2 * rows, n), :] = side_l[pl.ds(0, n), :]
    share[pl.ds(2 * rows + n, n), :] = side_r[pl.ds(0, n), :]
    size = share.shape[0]
    more = [
        pltpu.make_async_copy(share, box.at[pl.ds(g * size, size)], sems.at[g]) for g in range(groups)
    ]
    for c in more:
        c.start()
    for c in copies + more:
        c.wait()


def decode(codes):
    hi = jnp.floor(codes * (1.0 / CZ))
    z = codes - hi * CZ
    k = jnp.floor((hi + 0.5) * (1.0 / (CA * NR)))
    rest = hi - k * (CA * NR)
    a = jnp.floor((rest + 0.5) * (1.0 / NR))
    return k, a, rest - a * NR, z


def spread(ref, index, rows, chunk, lane_at=0, weigh=False):
    for first in range(0, rows, chunk):
        size = min(chunk, rows - first)
        near = jnp.clip(index - first, -1.0, 256.0)
        at = lax.broadcasted_iota(jnp.int32, (size, CZ), 0).astype(F32).astype(jnp.bfloat16)
        for i in range(index.shape[0]):
            w = jnp.full((size, CZ), 2.0 ** (-12 * (i // 4)) if weigh else 1.0, jnp.bfloat16)
            here = jnp.broadcast_to(near[i : i + 1, :], (size, CZ)).astype(jnp.bfloat16)
            ref[pl.ds(first, size), pl.ds(lane_at + i * CZ, CZ)] = jnp.where(
                at == here, w, jnp.zeros_like(w)
            )


def read_breaks(sz, parts, out, rows_ref, cols_ref, acc):
    for src, lo_group, groups, first, count, at in parts:
        k, a, r, z = decode(src)
        group = jnp.floor(a * 0.25)
        per_k = groups * NR
        rows = -(-NBOND * per_k // 16) * 16
        inside = (group >= lo_group) & (group < lo_group + groups)
        index = jnp.where(inside, k * per_k + (group - lo_group) * NR + r, -1.0)
        spread(rows_ref, index, rows, 240)
        spread(cols_ref, (a - 4 * group) * CZ + z, 4 * CZ, CZ * 2, weigh=True)
        acc[pl.ds(PAD, rows), :] = dot_nt(rows_ref[pl.ds(0, rows), :], cols_ref[...])
        for b in range(NBOND):
            for i in range(count):
                plane = first + i
                row = PAD + b * per_k + (plane // 4 - lo_group) * NR
                lanes = pl.ds(plane % 4 * CZ, CZ)
                out[b, at + i] = jnp.where(
                    is_top(), acc[pl.ds(row, PAIR), lanes], acc[pl.ds(row - NR, PAIR), lanes]
                )


def breaks_own(sz, codes, out, rows_ref, cols_ref, acc):
    acc[pl.ds(0, PAD), :] = jnp.zeros((PAD, 4 * CZ), F32)
    read_breaks(sz, [(codes[...], 0, CA // 4, 0, CA, 0)], out, rows_ref, cols_ref, acc)


def breaks_all(
    sz, at_lo, at_hi, side_l, side_r, own, low, high, box, out, rows_ref, cols_ref, acc, rows_s, cols_s, acc_l, acc_r
):
    n, halo = sz.code_rows, sz.halo
    acc[pl.ds(0, PAD), :] = jnp.zeros((PAD, 4 * CZ), F32)
    parts = [
        (low[...], (CA - halo) // 4, halo // 4, CA - halo, halo, 0),
        (high[...], 0, halo // 4, 0, halo, halo + CA),
    ]
    read_breaks(sz, parts, out, rows_ref, cols_ref, acc)
    wide = lanes_of((PAIR, CZ))
    edge = (is_top() & (wide >= CZ - SLOT)) | (~is_top() & (wide < SLOT))
    sources = [
        (box[pl.ds(at_lo, n), :], box[pl.ds(at_lo + n, n), :]),
        (side_l[pl.ds(0, n), :], side_r[pl.ds(0, n), :]),
        (box[pl.ds(at_hi, n), :], box[pl.ds(at_hi + n, n), :]),
    ]
    side_breaks(sz, sources, own, out, rows_s, cols_s, acc_l, acc_r, edge)


def side_breaks(sz, sources, own, out, rows_ref, cols_ref, acc_l, acc_r, edge):
    rows = -(-NBOND * NR // 16) * 16
    for which, (left, right) in enumerate(sources):
        first = CA - sz.halo if which == 0 else 0
        count = CA if which == 1 else sz.halo
        cols = -(-count // PER) * CZ
        for side, codes in enumerate((left, right)):
            k, a, r, z = decode(codes)
            spread(rows_ref, k * NR + r, rows, 192)
            a = a - first
            tile = jnp.floor(a * (1.0 / PER))
            slot = a - tile * PER + side
            slot = jnp.where(slot == PER, 0.0, slot)
            lane = z if side else z - (CZ - SLOT)
            near = (lane >= 0) & (lane < SLOT) & (a >= 0) & (a < count)
            spread(cols_ref, jnp.where(near, tile * CZ + slot * SLOT + lane, -1.0), cols, 256, weigh=True)
            acc = acc_r if side else acc_l
            acc[pl.ds(PAD, rows), pl.ds(0, cols)] = dot_nt(rows_ref[...], cols_ref[pl.ds(0, cols), :])
        for b in range(NBOND):
            for t in range(cols // CZ):
                lanes = pl.ds(t * CZ, CZ)
                x = jnp.where(
                    is_top(), acc_l[pl.ds(PAD + b * NR, PAIR), lanes], acc_r[pl.ds(PAD + b * NR - NR, PAIR), lanes]
                )
                for s in range(min(PER, count - t * PER)):
                    i = t * PER + s
                    p = i + (0, sz.halo, sz.halo + CA)[which]
                    old = own[b, i] if which == 1 else out[b, p]
                    out[b, p] = jnp.where(edge, roll(x, SLOT * (PER - 1 - s)), old)


def march(
    sz, total, held, place, side_l, side_r, disp, velo, stiff, low, high, ring_lo, ring_hi, owner, row_of,
    box, broken, out_d, out_v, out_e, fld, stiffk, heatk, bonds, forces, wait_a, wait_b, energy, pooled, temp, tables, heat3,
):
    refs = (disp, velo, stiff)
    halo = sz.halo
    lane = lanes_of()
    wide = lanes_of((PAIR, CZ))
    top = is_top()
    edge = (top & (wide >= CZ - SLOT)) | (~top & (wide < SLOT))
    share = 2 * (held + sz.code_rows)
    heat = box[...]
    wanted = (owner[...] * share + row_of[...]).astype(F32)
    wanted = exact_dot(jnp.broadcast_to(wanted, (8, wanted.shape[1])), layers_of(), ((1,), (1,)))
    lists = {
        (0, 1): low[pl.ds(sz.tab_at, 8), pl.ds(0, sz.table)],
        (1, 1): wanted,
        (2, 1): high[pl.ds(sz.tab_at, 8), pl.ds(0, sz.table)],
    }
    for which, ref, at in (
        (0, ring_lo, 0), (0, ring_lo, sz.side_rows), (1, side_l, 0), (1, side_r, 0), (2, ring_hi, 0), (2, ring_hi, sz.side_rows)
    ):
        side = 2 if at or ref is side_r else 0
        lists[which, side] = ref[pl.ds(at + sz.side_tab, 8), pl.ds(0, sz.table)] + held
    parts, rest = [], heat
    for _ in range(3):
        part = rest.astype(jnp.bfloat16)
        parts.append(part)
        rest = rest - part.astype(F32)
    for i, part in enumerate(parts):
        heat3[:, pl.ds(i * CZ, CZ)] = part
    for j, (key, table) in enumerate(lists.items()):
        tables[pl.ds(j, 1), pl.ds(0, sz.table)] = table[0:1]
    columns = tables[...].T
    row_id = lax.broadcasted_iota(jnp.int32, (sz.table, heat.shape[0]), 1).astype(F32)
    for j, (which, side) in enumerate(lists):
        hot = jnp.where(columns[0 : sz.table, j : j + 1] == row_id, 1.0, 0.0).astype(jnp.bfloat16)
        got = jnp.dot(hot, heat3[...], preferred_element_type=F32)
        temp[3 * which + side, pl.ds(PAD, sz.table), :] = (
            got[:, 0:CZ] + got[:, CZ : 2 * CZ] + got[:, 2 * CZ :]
        )
    for p in range(sz.ext):
        which, a = sz.source(p)
        for f in range(NFIELD):
            if which == 1:
                x = own_plane(refs, f, a)
                x = jnp.concatenate([x, x], axis=0)
                y = twice(side_l, side_r, sz.side_row(f, a // PER))
            else:
                at = sz.edge_row(f, p)
                if at is None:
                    continue
                src = low if which == 0 else high
                x = twice(src, src, at)
                ring = ring_lo if which == 0 else ring_hi
                at = sz.side_row(f, a // PER)
                y = twice(ring, ring, at, at + sz.side_rows)
            fld[f, p] = jnp.where(edge, roll(y, SLOT * (PER - 1 - a % PER)), x)
        at = PAD + a // 2 * NR
        x = twice(temp.at[3 * which + 1], temp.at[3 * which + 1], at)
        y = twice(temp.at[3 * which], temp.at[3 * which + 2], at)
        fld[NFIELD, p] = jnp.where(edge, y, x)

    row = lax.broadcasted_iota(jnp.int32, (PAIR, CZ), 0)
    not_top = jnp.where((row == NR - 1) | (row == PAIR - 1), 0.0, 1.0)
    start = place[0] * CA - halo

    def turned(cache, f, p, i, dz):
        key = f, i, dz
        if key not in cache:
            x = turned(cache, f, p, i, 0) if dz else fld[f, p + i]
            cache[key] = roll(x, -dz)
        return cache[key]

    def prepare(p):
        cache = {}
        get = lambda f, i, dz=0: turned(cache, f, p, i, dz)
        for i in range(PREPARE):
            at = start + p + i
            live = [
                jnp.where((at >= 0) & (at + da < total), 1.0, 0.0).astype(F32) for da in range(REACH + 1)
            ]
            c, h = get(6, i), get(7, i)
            for k, (da, dr, dz) in enumerate(OFFSETS):
                n2, d = scales((da, dr, dz))
                if dr:
                    c2, h2 = roll(c, -1, 0), roll(h, -1, 0)
                else:
                    c2, h2 = get(6, i + da, dz), get(7, i + da, dz)
                m = (c + c2) * (live[da] * (0.5 * d * d / (n2 * n2)))
                stiffk[k, p + i] = m * not_top if dr else m
                heatk[k, p + i] = (h + h2) * (DILATION * 0.5 * n2 / d)

    def several(body, first_plane, times, group=UNROLL):
        def one(i, c):
            body(first_plane + i * group)
            return c

        lax.fori_loop(0, times, one, 0)

    several(prepare, 0, (sz.ext - 1) // PREPARE, PREPARE)
    energy[...] = jnp.zeros_like(energy)

    span = range(UNROLL)

    def pull(p, limit, with_energy):
        cache = {}
        get = lambda f, i, dz=0: turned(cache, f, p, i, dz)
        fa_at = {i: wait_a[i] for i in range(REACH)}
        fz_at = {}
        sums = [{} for _ in span]
        keep = []

        def add(to, i, x):
            to[i] = to[i] + x if i in to else x

        def bond(i, o, elongation):
            k = NUMBER[o]
            q = elongation - heatk[k, p + i]
            g = jnp.where(broken[k, p + i] >= limit, 0.0, stiffk[k, p + i]) * q
            if with_energy:
                add(sums[i], scales(o)[0], g * q)
            if o[2]:
                keep.append((bonds, (k, i), g))
            return g

        for i in span:
            ua, ur, uz = get(0, i), get(1, i), get(2, i)
            for dz in (1, 2, 3):
                add(fz_at, i, bond(i, (0, 0, dz), get(2, i, dz) - uz))
            g = bond(i, (0, 1, 0), roll(ur, -1, 0) - ur)
            keep.append((forces, (1, i), g - roll(g, 1, 0)))
            for da in (1, 2):
                j = i + da
                g = bond(i, (da, 0, 0), get(0, j) - ua)
                add(fa_at, i, g)
                add(fa_at, j, -g)
                for dz in (1, 2):
                    gs = []
                    for sign in (1, -1):
                        dua = get(0, j, sign * dz) - ua
                        duz = get(2, j, sign * dz) - uz
                        if da == dz:
                            e = dua + duz if sign > 0 else dua - duz
                        elif dz == 2:
                            e = dua + (2.0 * sign) * duz
                        else:
                            e = 2.0 * dua + duz if sign > 0 else 2.0 * dua - duz
                        gs.append(bond(i, (da, 0, sign * dz), e))
                    own_s, own_d = gs[0] + gs[1], gs[0] - gs[1]
                    add(fa_at, i, own_s if da in (1, dz) else float(da) * own_s)
                    add(fz_at, i, own_d if dz in (1, da) else float(dz) * own_d)
            g = bond(i, (3, 0, 0), get(0, i + 3) - ua)
            add(fa_at, i, g)
            add(fa_at, i + 3, -g)
            keep.append((forces, (0, i), fa_at[i]))
            keep.append((forces, (2, i), fz_at[i]))
        keep += [(wait_a, (i,), fa_at[i + UNROLL]) for i in range(REACH)]
        if with_energy:
            for i in span:
                e = None
                for n2, x in sums[i].items():
                    y = x * (0.5 / math.sqrt(n2))
                    e = y if e is None else e + y
                keep.append((energy, (p + i - halo,), energy[p + i - halo] + e))
        return keep

    def push(p):
        fa_at = {i: wait_b[0, i] for i in range(REACH - 1)}
        fz_at = {i: wait_b[1, i] for i in range(REACH - 1)}
        keep = []

        def add(to, i, x):
            to[i] = to[i] + x if i in to else x

        for i in span:
            for da in (0, 1, 2):
                j = i + da
                for dz in (1, 2) if da else (1, 2, 3):
                    plus = roll(bonds[NUMBER[da, 0, dz], i], dz)
                    if da == 0:
                        add(fz_at, j, plus)
                        continue
                    minus = roll(bonds[NUMBER[da, 0, -dz], i], -dz)
                    both, gap = plus + minus, plus - minus
                    add(fa_at, j, both if da in (1, dz) else float(da) * both)
                    add(fz_at, j, gap if dz in (1, da) else float(dz) * gap)
            for f, force in (
                (0, forces[0, i] - fa_at[i]),
                (1, forces[1, i]),
                (2, forces[2, i] - fz_at[i]),
            ):
                v = fld[3 + f, p + i] + DT * force
                keep.append((fld, (3 + f, p + i), v))
                keep.append((fld, (f, p + i), fld[f, p + i] + DT * v))
        for i in range(REACH - 1):
            keep.append((wait_b, (0, i), fa_at[UNROLL + i]))
            keep.append((wait_b, (1, i), fz_at[UNROLL + i]))
        return keep

    def store(keep):
        for ref, index, value in keep:
            ref[index] = value

    def both_halves(limit, with_energy):
        def run(p):
            late = push(p - UNROLL)
            fresh = pull(p, limit, with_energy)
            store(fresh)
            store(late)

        return run

    counted = -(-CA // UNROLL)

    def step(s, limit):
        first_plane = REACH * s
        store(pull(first_plane, limit, False))
        quiet = both_halves(limit, False)
        several(quiet, first_plane + UNROLL, sz.sections - 1 - s)
        several(both_halves(limit, True), halo, counted)
        several(quiet, halo + counted * UNROLL, sz.sections - 1 - s)
        store(push(halo + (counted + sz.sections - 2 - s) * UNROLL))
        return limit * (2.0**-12)

    for ref in (wait_a, wait_b):
        ref[...] = jnp.zeros_like(ref)
    lax.fori_loop(0, sz.sections, step, jnp.float32(1.0))

    half = lane < CZ // 2
    for c in range(3):
        for a in range(CA):
            at = pl.ds(c * CA * NR + a, NR, stride=CA)
            p = halo + a
            out_d[at, :] = jnp.where(half, fld[c, p, pl.ds(0, NR), :], fld[c, p, pl.ds(NR, NR), :])
            out_v[at, :] = jnp.where(half, fld[3 + c, p, pl.ds(0, NR), :], fld[3 + c, p, pl.ds(NR, NR), :])
    for b in range(CA // 2):
        up = energy[2 * b, pl.ds(0, NR), :] + energy[2 * b + 1, pl.ds(0, NR), :]
        dn = energy[2 * b, pl.ds(NR, NR), :] + energy[2 * b + 1, pl.ds(NR, NR), :]
        pooled[pl.ds(b * NR, NR), :] = jnp.where(half, up, dn) * (0.25 / sz.sections)
    mean = exact_dot(layers_of(), pooled[...], ((0,), (0,)))
    table = owner[...] * held + row_of[...]
    out_e[...] = exact_dot(wanted_rows(table, out_e.shape[0]), mean)


def call(body, ins, outs, scratch=(), name=None, in_hbm=0):
    arrays, spaces, parts = [], [], []
    for i in ins:
        x, how = i if isinstance(i, tuple) else (i, i.shape[0])
        staged = isinstance(how, int)
        arrays.append(pltpu.with_memory_space_constraint(x, pltpu.HBM) if staged else x)
        spaces.append(pltpu.HBM if staged else how)
        parts.append(how if staged else None)
    staged = [i for i, m in enumerate(parts) if m is not None]
    buffers = [pltpu.VMEM((parts[i],) + arrays[i].shape[1:], arrays[i].dtype) for i in staged]

    def kernel(*refs):
        refs = list(refs)
        sems = refs.pop()
        held = refs[len(refs) - len(staged) :]
        refs = refs[: len(refs) - len(staged)]
        copies = [
            pltpu.make_async_copy(refs[i].at[pl.ds(0, parts[i])], held[j], sems.at[j])
            for j, i in enumerate(staged)
        ]
        for c in copies:
            c.start()
        for j, i in enumerate(staged):
            refs[i] = held[j]
        for c in copies:
            c.wait()
        body(*refs)

    every = list(scratch) + buffers
    size = sum(math.prod(b.shape) * 4 for b in every)
    size += sum(4 * math.prod(s) for s in outs)
    size += sum(4 * math.prod(a.shape) for a, m in zip(arrays, spaces) if m is pltpu.VMEM)
    return pl.pallas_call(
        kernel,
        name=name,
        out_shape=[
            pltpu.HBM(s, F32) if i >= len(outs) - in_hbm else jax.ShapeDtypeStruct(s, F32)
            for i, s in enumerate(outs)
        ],
        in_specs=[pl.BlockSpec(memory_space=m) for m in spaces],
        out_specs=[pl.BlockSpec(memory_space=pltpu.VMEM)] * (len(outs) - in_hbm)
        + [pl.BlockSpec(memory_space=pltpu.HBM)] * in_hbm,
        scratch_shapes=every + [pltpu.SemaphoreType.DMA((max(1, len(staged)),))],
        compiler_params=pltpu.CompilerParams(vmem_limit_bytes=min(60 << 20, size + (6 << 20))),
    )(*arrays)


def on_device(displace, velocity, stiff, thermal, owner_of, row_of, breaks):
    sz = Sizes(breaks.shape[0], thermal.shape[0])
    groups = lax.axis_size("axial")
    around = lax.axis_size("azim")
    held = thermal.shape[0]
    nreq = row_of.shape[-1]
    codes = breaks.reshape(sz.code_rows, CZ)
    owner = owner_of.reshape(1, nreq)
    local = row_of.reshape(1, nreq)
    disp = displace.transpose(0, 2, 1, 3).reshape(3 * NR * CA, CZ)
    velo = velocity.transpose(0, 2, 1, 3).reshape(3 * NR * CA, CZ)
    stif = stiff.transpose(1, 0, 2).reshape(NR * CA, CZ)

    edge, side = (sz.edge_rows, CZ), (sz.side_rows, CZ)
    n = sz.code_rows
    share = 2 * (held + n)
    up, down, left, right, code_f = call(
        lambda *refs: pack_first(sz, share, *refs),
        [disp, velo, stif, codes, owner, local, thermal],
        [edge, edge, side, side, (n, CZ)],
        name="pack_first",
    )
    to_left = [(i, (i - 1) % around) for i in range(around)]
    to_right = [(i, (i + 1) % around) for i in range(around)]
    upward = [(i, i + 1) for i in range(groups - 1)]
    downward = [(i + 1, i) for i in range(groups - 1)]
    side_r = lax.ppermute(left, "azim", to_left)
    side_l = lax.ppermute(right, "azim", to_right)
    low = lax.ppermute(up, "axial", upward)
    high = lax.ppermute(down, "axial", downward)
    plane = (PAIR, CZ)
    lanes = n * CZ
    tall = NBOND * CA // 4 * NR
    work = [
        pltpu.VMEM((tall, lanes), jnp.bfloat16),
        pltpu.VMEM((4 * CZ, lanes), jnp.bfloat16),
        pltpu.VMEM((tall + 2 * PAD, 4 * CZ), F32),
    ]
    (w_own,) = call(
        lambda *refs: breaks_own(sz, *refs),
        [(code_f, pltpu.VMEM)],
        [(NBOND, CA) + plane],
        work,
        name="breaks_own",
    )
    side_l, side_r, w_own = lax.optimization_barrier((side_l, side_r, w_own))
    ring, out_box = call(
        lambda *refs: relay(sz, groups, *refs),
        [thermal, (side_l, pltpu.VMEM), (side_r, pltpu.VMEM)],
        [(2 * sz.side_rows, CZ), (groups * share, CZ)],
        [pltpu.VMEM((share, CZ), F32), pltpu.SemaphoreType.DMA((groups,)), pltpu.SemaphoreType.DMA((2,))],
        name="relay",
        in_hbm=2,
    )
    ring_lo = lax.ppermute(ring, "axial", upward)
    ring_hi = lax.ppermute(ring, "axial", downward)
    box = lax.all_to_all(out_box.reshape(groups, share, CZ), "axial", split_axis=0, concat_axis=0, tiled=True)
    box = box.reshape(groups * share, CZ)
    strip = -(-NBOND * NR // 16) * 16
    place = lax.axis_index("axial").astype(jnp.int32).reshape(1)

    def all_breaks(place, *refs):
        x = place[0]
        rows = [
            pl.multiple_of(jnp.clip(x + d, 0, groups - 1) * share + 2 * held, 8) for d in (-1, 1)
        ]
        breaks_all(sz, *rows, *refs)

    (broken,) = call(
        all_breaks,
        [(place, pltpu.SMEM), (side_l, pltpu.VMEM), (side_r, pltpu.VMEM), (w_own, pltpu.VMEM), (low, n), (high, n), (box, pltpu.VMEM)],
        [(NBOND, sz.ext) + plane],
        work
        + [
            pltpu.VMEM((strip, lanes), jnp.bfloat16),
            pltpu.VMEM((CA * SLOT, lanes), jnp.bfloat16),
            pltpu.VMEM((strip + 2 * PAD, CA * SLOT), F32),
            pltpu.VMEM((strip + 2 * PAD, CA * SLOT), F32),
        ],
        name="breaks_all",
    )
    planes = sz.ext + 2
    scratch = [
        pltpu.VMEM((NFIELD + 1, planes) + plane, F32),
        pltpu.VMEM((NBOND, sz.ext) + plane, F32),
        pltpu.VMEM((NBOND, sz.ext) + plane, F32),
        pltpu.VMEM((NBOND, UNROLL) + plane, F32),
        pltpu.VMEM((3, UNROLL) + plane, F32),
        pltpu.VMEM((REACH,) + plane, F32),
        pltpu.VMEM((2, REACH - 1) + plane, F32),
        pltpu.VMEM((-(-CA // UNROLL) * UNROLL,) + plane, F32),
        pltpu.VMEM((CA // 2 * NR, CZ), F32),
        pltpu.VMEM((9, PAD + sz.table + PAD, CZ), F32),
        pltpu.VMEM((CZ, CZ), F32),
        pltpu.VMEM((groups * share, 3 * CZ), jnp.bfloat16),
    ]
    total = groups * CA
    out_d, out_v, out_e = call(
        lambda *refs: march(sz, total, held, *refs),
        [
            (place, pltpu.SMEM), (side_l, pltpu.VMEM), (side_r, pltpu.VMEM), disp, velo, stif, low, high, ring_lo, ring_hi, owner, local,
            (box, pltpu.VMEM), (broken, pltpu.VMEM),
        ],
        [disp.shape, velo.shape, (groups * held, CZ)],
        scratch,
        name="march",
    )
    parts = out_e.reshape(groups, held, CZ)
    arrived = lax.all_to_all(parts, "axial", split_axis=0, concat_axis=0, tiled=True)
    shape = (3, NR, CA, CZ)
    return (
        out_d.reshape(shape).transpose(0, 2, 1, 3),
        out_v.reshape(shape).transpose(0, 2, 1, 3),
        jnp.sum(arrived, axis=0),
    )


def solution(mesh):
    return jax.shard_map(
        on_device,
        mesh=mesh,
        in_specs=(
            P(None, "axial", None, "azim"),
            P(None, "axial", None, "azim"),
            P("axial", None, "azim"),
            P("axial", "azim"),
            P("axial", "azim", None, None),
            P("axial", "azim", None),
            P(None, "axial", "azim", None),
        ),
        out_specs=(
            P(None, "axial", None, "azim"),
            P(None, "axial", None, "azim"),
            P("axial", "azim"),
        ),
        check_vma=False,
    )
```

```python
import math

import jax
import jax.numpy as jnp
from jax import lax
from jax.experimental import pallas as pl
from jax.experimental.pallas import tpu as pltpu
from jax.sharding import PartitionSpec as P

DILATION = 0.25
DT = 0.2
CA, NR, CZ = 16, 12, 128
REACH = 3
SLOT = 16
PAIR = 2 * NR
PAD = 16
PER = CZ // SLOT
UNROLL = 3
PREPARE = 13
NFIELD = 7
NEXACT = lax.Precision.HIGHEST
F32 = jnp.float32


def offset_table():
    table = []
    for da in range(REACH + 1):
        for dz in range(-REACH, REACH + 1):
            if da * da + dz * dz <= REACH * REACH and (da > 0 or dz > 0):
                table.append((da, 0, dz))
    table.append((0, 1, 0))
    return table


OFFSETS = offset_table()
NBOND = len(OFFSETS)
NUMBER = {o: i for i, o in enumerate(OFFSETS)}


def scales(o):
    return sum(x * x for x in o), math.gcd(math.gcd(o[0], o[1]), abs(o[2]))


def roll(x, shift, axis=1):
    shift %= x.shape[axis]
    return pltpu.roll(x, shift, axis) if shift else x


def lanes_of(shape=(NR, CZ)):
    return lax.broadcasted_iota(jnp.int32, shape, 1)


def dot_nt(a, b):
    return lax.dot_general(a, b, (((1,), (1,)), ((), ())), preferred_element_type=F32)


class Sizes:
    def __init__(self, sections, rows):
        self.sections = sections
        self.halo = REACH * sections
        self.ext = CA + 2 * self.halo
        self.code_rows = 4 * sections
        self.edge_at = {}
        at = PAD
        for f in range(NFIELD):
            for e in range(self.halo):
                if not self.moving(f) or e < self.halo - REACH:
                    self.edge_at[f, e] = at
                    at += NR
        self.tab_at = -(-at // 8) * 8
        self.edge_rows = self.tab_at + PAD
        self.own_tiles = CA // PER
        self.side_heat = -(-(PAD + NFIELD * self.own_tiles * NR + NR) // 8) * 8
        self.side_tab = self.side_heat + rows
        self.side_rows = self.side_tab + 8
        self.table = CA // 2 * NR

    def moving(self, f):
        return 3 <= f < 6

    def edge_row(self, f, p):
        e = p if p < self.halo else p - self.halo - CA
        if self.moving(f) and p < self.halo:
            e -= REACH
        return self.edge_at.get((f, e))

    def source(self, p):
        if p < self.halo:
            return 0, CA - self.halo + p
        if p < self.halo + CA:
            return 1, p - self.halo
        return 2, p - self.halo - CA

    def side_row(self, f, t):
        return PAD + (f * self.own_tiles + t) * NR


def own_plane(refs, f, a):
    disp, velo, stiff = refs
    ref, g = (disp, f) if f < 3 else (velo, f - 3) if f < 6 else (stiff, 0)
    return ref[pl.ds(g * CA * NR + a, NR, stride=CA), :]


def is_top():
    return lax.broadcasted_iota(jnp.int32, (PAIR, CZ), 0) < NR


def twice(upper, lower, at, low_at=None):
    low_at = at if low_at is None else low_at
    return jnp.where(is_top(), upper[pl.ds(at, PAIR), :], lower[pl.ds(low_at - NR, PAIR), :])


def wanted_rows(table, count):
    rows = lax.broadcasted_iota(jnp.int32, (count, table.shape[1]), 0)
    return (rows == table).astype(F32)


def layers_of():
    shape = (CA // 2 * NR, CA // 2 * NR // 2)
    i = lax.broadcasted_iota(jnp.int32, shape, 0)
    j = lax.broadcasted_iota(jnp.int32, shape, 1)
    return (i // 2 == j).astype(F32)


def exact_dot(a, b, dims=((1,), (0,))):
    return lax.dot_general(a, b, (dims, ((), ())), precision=NEXACT, preferred_element_type=F32)


def pack_tiles(sz, planes, left, right, row):
    lane = lanes_of()
    to_left = to_right = None
    for s, x in enumerate(planes):
        if x is None:
            continue
        x = roll(x, SLOT * (s + 1))
        if to_left is None:
            to_left = to_right = x
            continue
        to_right = jnp.where(lane >= SLOT * s, x, to_right)
        n = (s + 1) % PER
        to_left = jnp.where((lane >= SLOT * n) & (lane < SLOT * (n + 1)), x, to_left)
    left[pl.ds(row, NR), :] = to_left
    right[pl.ds(row, NR), :] = to_right


def pack_first(sz, share, disp, velo, stiff, codes, owner, row_of, thermal, up, down, left, right, code_f):
    refs = (disp, velo, stiff)
    for f in range(NFIELD):
        for p in range(sz.halo):
            at = sz.edge_row(f, p)
            if at is not None:
                up[pl.ds(at, NR), :] = own_plane(refs, f, CA - sz.halo + p)
            at = sz.edge_row(f, p + sz.halo + CA)
            if at is not None:
                down[pl.ds(at, NR), :] = own_plane(refs, f, p)
        for t in range(sz.own_tiles):
            planes = [own_plane(refs, f, t * PER + s) for s in range(PER)]
            pack_tiles(sz, planes, left, right, sz.side_row(f, t))
    c = codes[...].astype(F32)
    code_f[...] = c
    wanted = (owner[...] * share + row_of[...]).astype(F32)
    wanted = jnp.broadcast_to(wanted, (8, wanted.shape[1]))
    table = exact_dot(wanted, layers_of(), ((1,), (1,)))
    for out in (up, down, left, right):
        out[pl.ds(0, sz.code_rows), :] = c
    for out, at in ((up, sz.tab_at), (down, sz.tab_at), (left, sz.side_tab), (right, sz.side_tab)):
        out[pl.ds(at, 8), pl.ds(0, sz.table)] = table
    for out in (left, right):
        out[pl.ds(sz.side_heat, thermal.shape[0]), :] = thermal[...]


def relay(sz, groups, thermal, side_l, side_r, ring, box, share, sems, ring_sems):
    rows = thermal.shape[0]
    n = sz.code_rows
    copies = [
        pltpu.make_async_copy(side, ring.at[pl.ds(i * sz.side_rows, sz.side_rows)], ring_sems.at[i])
        for i, side in enumerate((side_l, side_r))
    ]
    for c in copies:
        c.start()
    heat = pl.ds(sz.side_heat, rows)
    share[pl.ds(0, rows), :] = thermal[...]
    share[pl.ds(rows, rows), :] = jnp.where(
        lanes_of((rows, CZ)) < CZ // 2, side_r[heat, :], side_l[heat, :]
    )
    share[pl.ds(2 * rows, n), :] = side_l[pl.ds(0, n), :]
    share[pl.ds(2 * rows + n, n), :] = side_r[pl.ds(0, n), :]
    size = share.shape[0]
    more = [
        pltpu.make_async_copy(share, box.at[pl.ds(g * size, size)], sems.at[g]) for g in range(groups)
    ]
    for c in more:
        c.start()
    for c in copies + more:
        c.wait()


def decode(codes):
    hi = jnp.floor(codes * (1.0 / CZ))
    z = codes - hi * CZ
    k = jnp.floor((hi + 0.5) * (1.0 / (CA * NR)))
    rest = hi - k * (CA * NR)
    a = jnp.floor((rest + 0.5) * (1.0 / NR))
    return k, a, rest - a * NR, z


def spread(ref, index, rows, chunk, lane_at=0, weigh=False):
    for first in range(0, rows, chunk):
        size = min(chunk, rows - first)
        near = jnp.clip(index - first, -1.0, 256.0)
        at = lax.broadcasted_iota(jnp.int32, (size, CZ), 0).astype(F32).astype(jnp.bfloat16)
        for i in range(index.shape[0]):
            w = jnp.full((size, CZ), 2.0 ** (-12 * (i // 4)) if weigh else 1.0, jnp.bfloat16)
            here = jnp.broadcast_to(near[i : i + 1, :], (size, CZ)).astype(jnp.bfloat16)
            ref[pl.ds(first, size), pl.ds(lane_at + i * CZ, CZ)] = jnp.where(
                at == here, w, jnp.zeros_like(w)
            )


def read_breaks(sz, parts, out, rows_ref, cols_ref, acc):
    for src, lo_group, groups, first, count, at in parts:
        k, a, r, z = decode(src)
        group = jnp.floor(a * 0.25)
        per_k = groups * NR
        rows = -(-NBOND * per_k // 16) * 16
        inside = (group >= lo_group) & (group < lo_group + groups)
        index = jnp.where(inside, k * per_k + (group - lo_group) * NR + r, -1.0)
        spread(rows_ref, index, rows, 240)
        spread(cols_ref, (a - 4 * group) * CZ + z, 4 * CZ, CZ * 2, weigh=True)
        acc[pl.ds(PAD, rows), :] = dot_nt(rows_ref[pl.ds(0, rows), :], cols_ref[...])
        for b in range(NBOND):
            for i in range(count):
                plane = first + i
                row = PAD + b * per_k + (plane // 4 - lo_group) * NR
                lanes = pl.ds(plane % 4 * CZ, CZ)
                out[b, at + i] = jnp.where(
                    is_top(), acc[pl.ds(row, PAIR), lanes], acc[pl.ds(row - NR, PAIR), lanes]
                )


def breaks_own(sz, codes, out, rows_ref, cols_ref, acc):
    acc[pl.ds(0, PAD), :] = jnp.zeros((PAD, 4 * CZ), F32)
    read_breaks(sz, [(codes[...], 0, CA // 4, 0, CA, 0)], out, rows_ref, cols_ref, acc)


def breaks_all(
    sz, at_lo, at_hi, side_l, side_r, own, low, high, box, out, rows_ref, cols_ref, acc, rows_s, cols_s, acc_l, acc_r
):
    n, halo = sz.code_rows, sz.halo
    acc[pl.ds(0, PAD), :] = jnp.zeros((PAD, 4 * CZ), F32)
    parts = [
        (low[...], (CA - halo) // 4, halo // 4, CA - halo, halo, 0),
        (high[...], 0, halo // 4, 0, halo - REACH, halo + CA),
    ]
    read_breaks(sz, parts, out, rows_ref, cols_ref, acc)
    wide = lanes_of((PAIR, CZ))
    edge = (is_top() & (wide >= CZ - SLOT)) | (~is_top() & (wide < SLOT))
    sources = [
        (box[pl.ds(at_lo, n), :], box[pl.ds(at_lo + n, n), :]),
        (side_l[pl.ds(0, n), :], side_r[pl.ds(0, n), :]),
        (box[pl.ds(at_hi, n), :], box[pl.ds(at_hi + n, n), :]),
    ]
    side_breaks(sz, sources, own, out, rows_s, cols_s, acc_l, acc_r, edge)


def side_breaks(sz, sources, own, out, rows_ref, cols_ref, acc_l, acc_r, edge):
    rows = -(-NBOND * NR // 16) * 16
    for which, (left, right) in enumerate(sources):
        first = CA - sz.halo if which == 0 else 0
        count = (sz.halo, CA, sz.halo - REACH)[which]
        cols = -(-count // PER) * CZ
        for side, codes in enumerate((left, right)):
            k, a, r, z = decode(codes)
            spread(rows_ref, k * NR + r, rows, 192)
            a = a - first
            tile = jnp.floor(a * (1.0 / PER))
            slot = a - tile * PER + side
            slot = jnp.where(slot == PER, 0.0, slot)
            lane = z if side else z - (CZ - SLOT)
            near = (lane >= 0) & (lane < SLOT) & (a >= 0) & (a < count)
            spread(cols_ref, jnp.where(near, tile * CZ + slot * SLOT + lane, -1.0), cols, 256, weigh=True)
            acc = acc_r if side else acc_l
            acc[pl.ds(PAD, rows), pl.ds(0, cols)] = dot_nt(rows_ref[...], cols_ref[pl.ds(0, cols), :])
        for b in range(NBOND):
            for t in range(cols // CZ):
                lanes = pl.ds(t * CZ, CZ)
                x = jnp.where(
                    is_top(), acc_l[pl.ds(PAD + b * NR, PAIR), lanes], acc_r[pl.ds(PAD + b * NR - NR, PAIR), lanes]
                )
                for s in range(min(PER, count - t * PER)):
                    i = t * PER + s
                    p = i + (0, sz.halo, sz.halo + CA)[which]
                    old = own[b, i] if which == 1 else out[b, p]
                    out[b, p] = jnp.where(edge, roll(x, SLOT * (PER - 1 - s)), old)


def march(
    sz, total, held, place, side_l, side_r, disp, velo, stiff, low, high, ring_lo, ring_hi, owner, row_of,
    box, broken, out_d, out_v, out_e, fld, stiffk, heatk, bonds, forces, wait_a, wait_b, energy, pooled, temp, tables, heat3,
):
    refs = (disp, velo, stiff)
    halo = sz.halo
    lane = lanes_of()
    wide = lanes_of((PAIR, CZ))
    top = is_top()
    edge = (top & (wide >= CZ - SLOT)) | (~top & (wide < SLOT))
    share = 2 * (held + sz.code_rows)
    heat = box[...]
    wanted = (owner[...] * share + row_of[...]).astype(F32)
    wanted = exact_dot(jnp.broadcast_to(wanted, (8, wanted.shape[1])), layers_of(), ((1,), (1,)))
    lists = {
        (0, 1): low[pl.ds(sz.tab_at, 8), pl.ds(0, sz.table)],
        (1, 1): wanted,
        (2, 1): high[pl.ds(sz.tab_at, 8), pl.ds(0, sz.table)],
    }
    for which, ref, at in (
        (0, ring_lo, 0), (0, ring_lo, sz.side_rows), (1, side_l, 0), (1, side_r, 0), (2, ring_hi, 0), (2, ring_hi, sz.side_rows)
    ):
        side = 2 if at or ref is side_r else 0
        lists[which, side] = ref[pl.ds(at + sz.side_tab, 8), pl.ds(0, sz.table)] + held
    parts, rest = [], heat
    for _ in range(3):
        part = rest.astype(jnp.bfloat16)
        parts.append(part)
        rest = rest - part.astype(F32)
    for i, part in enumerate(parts):
        heat3[:, pl.ds(i * CZ, CZ)] = part
    for j, (key, table) in enumerate(lists.items()):
        tables[pl.ds(j, 1), pl.ds(0, sz.table)] = table[0:1]
    columns = tables[...].T
    row_id = lax.broadcasted_iota(jnp.int32, (sz.table, heat.shape[0]), 1).astype(F32)
    for j, (which, side) in enumerate(lists):
        hot = jnp.where(columns[0 : sz.table, j : j + 1] == row_id, 1.0, 0.0).astype(jnp.bfloat16)
        got = jnp.dot(hot, heat3[...], preferred_element_type=F32)
        temp[3 * which + side, pl.ds(PAD, sz.table), :] = (
            got[:, 0:CZ] + got[:, CZ : 2 * CZ] + got[:, 2 * CZ :]
        )
    for p in range(sz.ext):
        which, a = sz.source(p)
        for f in range(NFIELD):
            if which == 1:
                x = own_plane(refs, f, a)
                x = jnp.concatenate([x, x], axis=0)
                y = twice(side_l, side_r, sz.side_row(f, a // PER))
            else:
                at = sz.edge_row(f, p)
                if at is None:
                    continue
                src = low if which == 0 else high
                x = twice(src, src, at)
                ring = ring_lo if which == 0 else ring_hi
                at = sz.side_row(f, a // PER)
                y = twice(ring, ring, at, at + sz.side_rows)
            fld[f, p] = jnp.where(edge, roll(y, SLOT * (PER - 1 - a % PER)), x)
        at = PAD + a // 2 * NR
        x = twice(temp.at[3 * which + 1], temp.at[3 * which + 1], at)
        y = twice(temp.at[3 * which], temp.at[3 * which + 2], at)
        fld[NFIELD, p] = jnp.where(edge, y, x)

    row = lax.broadcasted_iota(jnp.int32, (PAIR, CZ), 0)
    not_top = jnp.where((row == NR - 1) | (row == PAIR - 1), 0.0, 1.0)
    start = place[0] * CA - halo

    def turned(cache, f, p, i, dz):
        key = f, i, dz
        if key not in cache:
            x = turned(cache, f, p, i, 0) if dz else fld[f, p + i]
            cache[key] = roll(x, -dz)
        return cache[key]

    def prepare(p):
        cache = {}
        get = lambda f, i, dz=0: turned(cache, f, p, i, dz)
        for i in range(PREPARE):
            at = start + p + i
            live = [
                jnp.where((at >= 0) & (at + da < total), 1.0, 0.0).astype(F32) for da in range(REACH + 1)
            ]
            c, h = get(6, i), get(7, i)
            for k, (da, dr, dz) in enumerate(OFFSETS):
                n2, d = scales((da, dr, dz))
                if dr:
                    c2, h2 = roll(c, -1, 0), roll(h, -1, 0)
                else:
                    c2, h2 = get(6, i + da, dz), get(7, i + da, dz)
                m = (c + c2) * (live[da] * (0.5 * d * d / (n2 * n2)))
                stiffk[k, p + i] = m * not_top if dr else m
                heatk[k, p + i] = (h + h2) * (DILATION * 0.5 * n2 / d)

    def several(body, first_plane, times, group=UNROLL):
        def one(i, c):
            body(first_plane + i * group)
            return c

        lax.fori_loop(0, times, one, 0)

    several(prepare, 0, (sz.ext - 1) // PREPARE, PREPARE)
    energy[...] = jnp.zeros_like(energy)

    span = range(UNROLL)

    def pull(p, limit, with_energy):
        cache = {}
        get = lambda f, i, dz=0: turned(cache, f, p, i, dz)
        fa_at = {i: wait_a[i] for i in range(REACH)}
        fz_at = {}
        sums = [{} for _ in span]
        keep = []

        def add(to, i, x):
            to[i] = to[i] + x if i in to else x

        def bond(i, o, elongation):
            k = NUMBER[o]
            q = elongation - heatk[k, p + i]
            g = jnp.where(broken[k, p + i] >= limit, 0.0, stiffk[k, p + i]) * q
            if with_energy:
                add(sums[i], scales(o)[0], g * q)
            if o[2]:
                keep.append((bonds, (k, i), g))
            return g

        for i in span:
            ua, ur, uz = get(0, i), get(1, i), get(2, i)
            for dz in (1, 2, 3):
                add(fz_at, i, bond(i, (0, 0, dz), get(2, i, dz) - uz))
            g = bond(i, (0, 1, 0), roll(ur, -1, 0) - ur)
            keep.append((forces, (1, i), g - roll(g, 1, 0)))
            for da in (1, 2):
                j = i + da
                g = bond(i, (da, 0, 0), get(0, j) - ua)
                add(fa_at, i, g)
                add(fa_at, j, -g)
                for dz in (1, 2):
                    gs = []
                    for sign in (1, -1):
                        dua = get(0, j, sign * dz) - ua
                        duz = get(2, j, sign * dz) - uz
                        if da == dz:
                            e = dua + duz if sign > 0 else dua - duz
                        elif dz == 2:
                            e = dua + (2.0 * sign) * duz
                        else:
                            e = 2.0 * dua + duz if sign > 0 else 2.0 * dua - duz
                        gs.append(bond(i, (da, 0, sign * dz), e))
                    own_s, own_d = gs[0] + gs[1], gs[0] - gs[1]
                    add(fa_at, i, own_s if da in (1, dz) else float(da) * own_s)
                    add(fz_at, i, own_d if dz in (1, da) else float(dz) * own_d)
            g = bond(i, (3, 0, 0), get(0, i + 3) - ua)
            add(fa_at, i, g)
            add(fa_at, i + 3, -g)
            keep.append((forces, (0, i), fa_at[i]))
            keep.append((forces, (2, i), fz_at[i]))
        keep += [(wait_a, (i,), fa_at[i + UNROLL]) for i in range(REACH)]
        if with_energy:
            for i in span:
                e = None
                for n2, x in sums[i].items():
                    y = x * (0.5 / math.sqrt(n2))
                    e = y if e is None else e + y
                keep.append((energy, (p + i - halo,), energy[p + i - halo] + e))
        return keep

    def push(p):
        fa_at = {i: wait_b[0, i] for i in range(REACH - 1)}
        fz_at = {i: wait_b[1, i] for i in range(REACH - 1)}
        keep = []

        def add(to, i, x):
            to[i] = to[i] + x if i in to else x

        for i in span:
            for da in (0, 1, 2):
                j = i + da
                for dz in (1, 2) if da else (1, 2, 3):
                    plus = roll(bonds[NUMBER[da, 0, dz], i], dz)
                    if da == 0:
                        add(fz_at, j, plus)
                        continue
                    minus = roll(bonds[NUMBER[da, 0, -dz], i], -dz)
                    both, gap = plus + minus, plus - minus
                    add(fa_at, j, both if da in (1, dz) else float(da) * both)
                    add(fz_at, j, gap if dz in (1, da) else float(dz) * gap)
            for f, force in (
                (0, forces[0, i] - fa_at[i]),
                (1, forces[1, i]),
                (2, forces[2, i] - fz_at[i]),
            ):
                v = fld[3 + f, p + i] + DT * force
                keep.append((fld, (3 + f, p + i), v))
                keep.append((fld, (f, p + i), fld[f, p + i] + DT * v))
        for i in range(REACH - 1):
            keep.append((wait_b, (0, i), fa_at[UNROLL + i]))
            keep.append((wait_b, (1, i), fz_at[UNROLL + i]))
        return keep

    def store(keep):
        for ref, index, value in keep:
            ref[index] = value

    def both_halves(limit, with_energy):
        def run(p):
            late = push(p - UNROLL)
            fresh = pull(p, limit, with_energy)
            store(fresh)
            store(late)

        return run

    counted = -(-CA // UNROLL)

    def step(s, limit):
        first_plane = REACH * s
        store(pull(first_plane, limit, False))
        quiet = both_halves(limit, False)
        several(quiet, first_plane + UNROLL, sz.sections - 1 - s)
        several(both_halves(limit, True), halo, counted)
        several(quiet, halo + counted * UNROLL, sz.sections - 1 - s)
        store(push(halo + (counted + sz.sections - 2 - s) * UNROLL))
        return limit * (2.0**-12)

    for ref in (wait_a, wait_b):
        ref[...] = jnp.zeros_like(ref)
    lax.fori_loop(0, sz.sections, step, jnp.float32(1.0))

    half = lane < CZ // 2
    for c in range(3):
        for a in range(CA):
            at = pl.ds(c * CA * NR + a, NR, stride=CA)
            p = halo + a
            out_d[at, :] = jnp.where(half, fld[c, p, pl.ds(0, NR), :], fld[c, p, pl.ds(NR, NR), :])
            out_v[at, :] = jnp.where(half, fld[3 + c, p, pl.ds(0, NR), :], fld[3 + c, p, pl.ds(NR, NR), :])
    for b in range(CA // 2):
        up = energy[2 * b, pl.ds(0, NR), :] + energy[2 * b + 1, pl.ds(0, NR), :]
        dn = energy[2 * b, pl.ds(NR, NR), :] + energy[2 * b + 1, pl.ds(NR, NR), :]
        pooled[pl.ds(b * NR, NR), :] = jnp.where(half, up, dn) * (0.25 / sz.sections)
    mean = exact_dot(layers_of(), pooled[...], ((0,), (0,)))
    table = owner[...] * held + row_of[...]
    out_e[...] = exact_dot(wanted_rows(table, out_e.shape[0]), mean)


def call(body, ins, outs, scratch=(), name=None, in_hbm=0):
    arrays, spaces, parts = [], [], []
    for i in ins:
        x, how = i if isinstance(i, tuple) else (i, i.shape[0])
        staged = isinstance(how, int)
        arrays.append(pltpu.with_memory_space_constraint(x, pltpu.HBM) if staged else x)
        spaces.append(pltpu.HBM if staged else how)
        parts.append(how if staged else None)
    staged = [i for i, m in enumerate(parts) if m is not None]
    buffers = [pltpu.VMEM((parts[i],) + arrays[i].shape[1:], arrays[i].dtype) for i in staged]

    def kernel(*refs):
        refs = list(refs)
        sems = refs.pop()
        held = refs[len(refs) - len(staged) :]
        refs = refs[: len(refs) - len(staged)]
        copies = [
            pltpu.make_async_copy(refs[i].at[pl.ds(0, parts[i])], held[j], sems.at[j])
            for j, i in enumerate(staged)
        ]
        for c in copies:
            c.start()
        for j, i in enumerate(staged):
            refs[i] = held[j]
        for c in copies:
            c.wait()
        body(*refs)

    every = list(scratch) + buffers
    size = sum(math.prod(b.shape) * 4 for b in every)
    size += sum(4 * math.prod(s) for s in outs)
    size += sum(4 * math.prod(a.shape) for a, m in zip(arrays, spaces) if m is pltpu.VMEM)
    return pl.pallas_call(
        kernel,
        name=name,
        out_shape=[
            pltpu.HBM(s, F32) if i >= len(outs) - in_hbm else jax.ShapeDtypeStruct(s, F32)
            for i, s in enumerate(outs)
        ],
        in_specs=[pl.BlockSpec(memory_space=m) for m in spaces],
        out_specs=[pl.BlockSpec(memory_space=pltpu.VMEM)] * (len(outs) - in_hbm)
        + [pl.BlockSpec(memory_space=pltpu.HBM)] * in_hbm,
        scratch_shapes=every + [pltpu.SemaphoreType.DMA((max(1, len(staged)),))],
        compiler_params=pltpu.CompilerParams(vmem_limit_bytes=min(60 << 20, size + (6 << 20))),
    )(*arrays)


def on_device(displace, velocity, stiff, thermal, owner_of, row_of, breaks):
    sz = Sizes(breaks.shape[0], thermal.shape[0])
    groups = lax.axis_size("axial")
    around = lax.axis_size("azim")
    held = thermal.shape[0]
    nreq = row_of.shape[-1]
    codes = breaks.reshape(sz.code_rows, CZ)
    owner = owner_of.reshape(1, nreq)
    local = row_of.reshape(1, nreq)
    disp = displace.transpose(0, 2, 1, 3).reshape(3 * NR * CA, CZ)
    velo = velocity.transpose(0, 2, 1, 3).reshape(3 * NR * CA, CZ)
    stif = stiff.transpose(1, 0, 2).reshape(NR * CA, CZ)

    edge, side = (sz.edge_rows, CZ), (sz.side_rows, CZ)
    n = sz.code_rows
    share = 2 * (held + n)
    up, down, left, right, code_f = call(
        lambda *refs: pack_first(sz, share, *refs),
        [disp, velo, stif, codes, owner, local, thermal],
        [edge, edge, side, side, (n, CZ)],
        name="pack_first",
    )
    to_left = [(i, (i - 1) % around) for i in range(around)]
    to_right = [(i, (i + 1) % around) for i in range(around)]
    upward = [(i, i + 1) for i in range(groups - 1)]
    downward = [(i + 1, i) for i in range(groups - 1)]
    side_r = lax.ppermute(left, "azim", to_left)
    side_l = lax.ppermute(right, "azim", to_right)
    low = lax.ppermute(up, "axial", upward)
    high = lax.ppermute(down, "axial", downward)
    plane = (PAIR, CZ)
    lanes = n * CZ
    tall = NBOND * CA // 4 * NR
    work = [
        pltpu.VMEM((tall, lanes), jnp.bfloat16),
        pltpu.VMEM((4 * CZ, lanes), jnp.bfloat16),
        pltpu.VMEM((tall + 2 * PAD, 4 * CZ), F32),
    ]
    (w_own,) = call(
        lambda *refs: breaks_own(sz, *refs),
        [(code_f, pltpu.VMEM)],
        [(NBOND, CA) + plane],
        work,
        name="breaks_own",
    )
    side_l, side_r, w_own = lax.optimization_barrier((side_l, side_r, w_own))
    ring, out_box = call(
        lambda *refs: relay(sz, groups, *refs),
        [thermal, (side_l, pltpu.VMEM), (side_r, pltpu.VMEM)],
        [(2 * sz.side_rows, CZ), (groups * share, CZ)],
        [pltpu.VMEM((share, CZ), F32), pltpu.SemaphoreType.DMA((groups,)), pltpu.SemaphoreType.DMA((2,))],
        name="relay",
        in_hbm=2,
    )
    ring_lo = lax.ppermute(ring, "axial", upward)
    ring_hi = lax.ppermute(ring, "axial", downward)
    box = lax.all_to_all(out_box.reshape(groups, share, CZ), "axial", split_axis=0, concat_axis=0, tiled=True)
    box = box.reshape(groups * share, CZ)
    strip = -(-NBOND * NR // 16) * 16
    place = lax.axis_index("axial").astype(jnp.int32).reshape(1)

    def all_breaks(place, *refs):
        x = place[0]
        rows = [
            pl.multiple_of(jnp.clip(x + d, 0, groups - 1) * share + 2 * held, 8) for d in (-1, 1)
        ]
        breaks_all(sz, *rows, *refs)

    (broken,) = call(
        all_breaks,
        [(place, pltpu.SMEM), (side_l, pltpu.VMEM), (side_r, pltpu.VMEM), (w_own, pltpu.VMEM), (low, n), (high, n), (box, pltpu.VMEM)],
        [(NBOND, sz.ext) + plane],
        work
        + [
            pltpu.VMEM((strip, lanes), jnp.bfloat16),
            pltpu.VMEM((CA * SLOT, lanes), jnp.bfloat16),
            pltpu.VMEM((strip + 2 * PAD, CA * SLOT), F32),
            pltpu.VMEM((strip + 2 * PAD, CA * SLOT), F32),
        ],
        name="breaks_all",
    )
    planes = sz.ext + 2
    scratch = [
        pltpu.VMEM((NFIELD + 1, planes) + plane, F32),
        pltpu.VMEM((NBOND, sz.ext) + plane, F32),
        pltpu.VMEM((NBOND, sz.ext) + plane, F32),
        pltpu.VMEM((NBOND, UNROLL) + plane, F32),
        pltpu.VMEM((3, UNROLL) + plane, F32),
        pltpu.VMEM((REACH,) + plane, F32),
        pltpu.VMEM((2, REACH - 1) + plane, F32),
        pltpu.VMEM((-(-CA // UNROLL) * UNROLL,) + plane, F32),
        pltpu.VMEM((CA // 2 * NR, CZ), F32),
        pltpu.VMEM((9, PAD + sz.table + PAD, CZ), F32),
        pltpu.VMEM((CZ, CZ), F32),
        pltpu.VMEM((groups * share, 3 * CZ), jnp.bfloat16),
    ]
    total = groups * CA
    out_d, out_v, out_e = call(
        lambda *refs: march(sz, total, held, *refs),
        [
            (place, pltpu.SMEM), (side_l, pltpu.VMEM), (side_r, pltpu.VMEM), disp, velo, stif, low, high, ring_lo, ring_hi, owner, local,
            (box, pltpu.VMEM), (broken, pltpu.VMEM),
        ],
        [disp.shape, velo.shape, (groups * held, CZ)],
        scratch,
        name="march",
    )
    parts = out_e.reshape(groups, held, CZ)
    arrived = lax.all_to_all(parts, "axial", split_axis=0, concat_axis=0, tiled=True)
    shape = (3, NR, CA, CZ)
    return (
        out_d.reshape(shape).transpose(0, 2, 1, 3),
        out_v.reshape(shape).transpose(0, 2, 1, 3),
        jnp.sum(arrived, axis=0),
    )


def solution(mesh):
    return jax.shard_map(
        on_device,
        mesh=mesh,
        in_specs=(
            P(None, "axial", None, "azim"),
            P(None, "axial", None, "azim"),
            P("axial", None, "azim"),
            P("axial", "azim"),
            P("axial", "azim", None, None),
            P("axial", "azim", None),
            P(None, "axial", "azim", None),
        ),
        out_specs=(
            P(None, "axial", None, "azim"),
            P(None, "axial", None, "azim"),
            P("axial", "azim"),
        ),
        check_vma=False,
    )
```
